32 devices in a mesh: group: 2 (over y), ctx: 4 (over z), head: 4 (over x, core).
Axes of the slice: x: 2, y: 2, z: 4, core: 2. Of those that a mesh axis runs over, the one named last changes fastest.
Arguments:
- head_input: bfloat16 [4096, 8192], P(('group', 'ctx'), 'head'), parts along dimension 0, may hold values from -6 to 6
- gate_input: bfloat16 [4096, 8192], P(('group', 'ctx'), 'head'), parts along dimension 0, may hold values from -40 to 40
- input_map: bfloat16 [4096, 2048], P(('group', 'ctx'), 'head'), parts along dimension 0, may hold values from -4 to 4
- output_map: bfloat16 [4096, 2048], P(('group', 'ctx'), 'head'), parts along dimension 0, may hold values from -4 to 4
- step_size: float32 [128, 4096], P('head', ('group', 'ctx')), parts along dimension 1, may hold values from 0.1 to 0.4
- decays: float32 [128, 4096], P('head', ('group', 'ctx')), parts along dimension 1, may hold values from 0.45 to 1
- bypass_scale: float32 [128], P('head'), may hold values from 1 to 4
- norm_gain: bfloat16 [8192], P('head'), may hold values from 0.099609375 to 1.8984375
- out_weight: bfloat16 [8192, 4096], P('head', 'ctx'), may hold values from -0.0625 to 0.0625
Outputs:
- layer_out: bfloat16 [4096, 4096], P(('group', 'ctx', 'head')), parts along dimension 0
The draws below stay inside these ranges and needn't reach their ends.
There are 2 independent parts, one for each index of `group`. The reference program is written for one: setup_inputs(seed, part) draws one part's arguments, and reference() takes and returns one part's arrays. A program takes and returns all parts, laid end to end along the dimension named above; an argument that names none is the same for every part. Nothing has to cross between parts.
All inputs are finite; a program needn't handle non-finite values.
Results may differ from the reference program's by a relative error of at most 0.014.
Values may be sent and summed in bfloat16 or wider, within the bound.
A program may use at most 128 MiB of HBM per device.

```python
import math
import jax
import jax.numpy as jnp
from jax import lax

HEADS = 128
HEADP = 64
STATE = 256
GROUPS = 8
DOUT = 4096
STRETCH = 128
TOKENS = 2048
N_HEAD = 4


def draw_decays(key, part):
    keys = jax.random.split(key, 6)
    fast_share = 0.5
    fast = jax.random.uniform(keys[0], (HEADS,)) < fast_share
    fast_rate = jnp.exp(jax.random.uniform(keys[1], (HEADS,), jnp.float32, math.log(1.0 / 50.0), math.log(1.0 / 30.0)))
    slow_rate = jnp.exp(jax.random.uniform(keys[2], (HEADS,), jnp.float32, math.log(0.01), math.log(0.3))) / TOKENS
    fading_speed = jnp.where(fast, fast_rate, slow_rate)
    approximate_guess = jnp.exp(jax.random.uniform(keys[3], (HEADS, TOKENS), jnp.float32, math.log(0.5), math.log(2.0)))
    spots = jax.random.randint(keys[4], (2,), 0, TOKENS)
    places = jnp.arange(TOKENS)
    masked_cells = (places == spots[0]) | (places == spots[1])
    fading_logs = jax.random.uniform(keys[5], (HEADS, 1), jnp.float32, 0.5, 0.8)
    segment_size = jnp.where(masked_cells[None, :], fading_logs, 1.0)
    return (jnp.exp(-fading_speed[:, None] * approximate_guess) * segment_size).astype(jnp.float32)


def draw_gate_input(key, part):
    keys = jax.random.split(key, 3)
    width = HEADS * HEADP
    base = jnp.clip(jax.random.normal(keys[0], (TOKENS, width), jnp.float32), -4.0, 4.0)
    column = jnp.exp(jax.random.uniform(keys[1], (width,), jnp.float32, math.log(0.3), math.log(3.0)))
    row = jnp.exp(jax.random.uniform(keys[2], (TOKENS, 1), jnp.float32, 0.0, math.log(3.0)))
    return (base * column[None, :] * row).astype(jnp.bfloat16)


def block_levels(stream_key, shape, cuts, low, high):
    gain, own = 1.0, jax.random.fold_in(stream_key, 6)
    for position, parts in cuts:
        heights = jnp.exp(jax.random.uniform(jax.random.fold_in(own, position), (parts,), jnp.float32, low / len(cuts), high / len(cuts)))
        gain = gain * jnp.repeat(heights, shape[position] // parts).reshape([-1 if axis == position else 1 for axis in range(len(shape))])
    return gain


def gaussian(rng, dims, deviation, reach, pieces=(), kind=jnp.bfloat16):
    loudness = block_levels(rng, dims, pieces, -0.22, 0.18) if pieces else 1.0
    entries = jax.random.normal(rng, dims, jnp.float32) * deviation * loudness
    return jnp.minimum(jnp.maximum(entries, -reach), reach).astype(kind)


def setup_inputs(seed: int = 0, part: int = 0) -> dict:
    arg_keys = jax.random.split(jax.random.key(seed), 10)
    own_keys = jax.random.split(jax.random.fold_in(arg_keys[9], part), 10)
    return {
        "head_input": gaussian(own_keys[0], (TOKENS, HEADS * HEADP), 1.0, 6.0, ((0, 4), (1, 4))),
        "gate_input": draw_gate_input(jax.random.fold_in(jax.random.fold_in(arg_keys[9], part), 71), part),
        "input_map": gaussian(own_keys[2], (TOKENS, GROUPS * STATE), 0.3, 4.0, ((0, 4), (1, 4))),
        "output_map": gaussian(own_keys[3], (TOKENS, GROUPS * STATE), 0.3, 4.0, ((0, 4), (1, 4))),
        "step_size": jnp.clip(jnp.exp(math.log(0.4) - 1.3862944 * jax.random.uniform(own_keys[4], (HEADS, TOKENS), jnp.float32) ** block_levels(own_keys[4], (HEADS, TOKENS), ((0, 4), (1, 4)), -0.2, 0.2)), 0.1, 0.4),
        "decays": draw_decays(jax.random.fold_in(jax.random.fold_in(arg_keys[9], part), 71), part),
        "bypass_scale": jnp.clip(jnp.exp(math.log(4.0) - 1.3862944 * jax.random.uniform(arg_keys[6], (HEADS,), jnp.float32) ** block_levels(arg_keys[6], (HEADS,), ((0, 4),), -0.2, 0.2)), 1.0, 4.0),
        "norm_gain": jnp.clip(1.0 + 0.18 * jax.random.normal(arg_keys[7], (HEADS * HEADP,), jnp.float32), 0.099609375, 1.8984375).astype(jnp.bfloat16),
        "out_weight": gaussian(arg_keys[8], (HEADS * HEADP, DOUT), (HEADS * HEADP) ** -0.5, 0.0625, ((0, 4), (1, 4))),
    }


def block_term_values(inputs, in_maps, out_maps, steps, decays):
    count, length, groups, per_group, channels = inputs.shape
    ramps = jnp.cumsum(jnp.log(decays), axis=-1)
    rows = lax.broadcasted_iota(jnp.int32, (length, length), 0)
    cols = lax.broadcasted_iota(jnp.int32, (length, length), 1)
    lower = rows >= cols
    spread = ramps[:, :, :, None] - ramps[:, :, None, :]
    within_decay = jnp.where(lower, jnp.exp(jnp.where(lower, spread, 0.0)), 0.0)
    scores = jnp.einsum('kqgn,ksgn->kgqs', out_maps.astype(jnp.float32), in_maps.astype(jnp.float32))
    mixing = within_decay.reshape(count, groups, per_group, length, length) * scores[:, :, None]
    mixing = mixing * steps.reshape(count, groups, per_group, 1, length)
    mixing = mixing.astype(jnp.bfloat16)
    within = jnp.einsum('kgjqs,ksgjp->kqgjp', mixing.astype(jnp.float32), inputs.astype(jnp.float32))
    tails = jnp.exp(ramps[:, :, -1:] - ramps) * steps
    tails = jnp.transpose(tails.reshape(count, groups, per_group, length), (0, 3, 1, 2))[..., None]
    weighted = (inputs.astype(jnp.float32) * tails).astype(jnp.bfloat16)
    block_state = jnp.einsum('ksgjp,ksgn->kgjpn', weighted.astype(jnp.float32), in_maps.astype(jnp.float32))
    accumulated_sums_list = jnp.exp(ramps[:, :, -1]).reshape(count, groups, per_group)
    entry = jnp.transpose(jnp.exp(ramps).reshape(count, groups, per_group, length), (0, 3, 1, 2))[..., None]
    return (within, block_state, accumulated_sums_list, entry)

def carried_terms(out_maps, entering, entry):
    carried = jnp.einsum('kqgn,kgjpn->kqgjp', out_maps.astype(jnp.float32), entering, precision=lax.Precision.HIGHEST)
    return carried * entry

def reference(head_input, gate_input, input_map, output_map, step_size, decays, bypass_scale, norm_gain, out_weight):
    per_group = HEADS // GROUPS
    blocks = TOKENS // STRETCH
    inputs = head_input.reshape(blocks, 1, STRETCH, GROUPS, per_group, HEADP)
    in_maps = input_map.reshape(blocks, 1, STRETCH, GROUPS, STATE)
    out_maps = output_map.reshape(blocks, 1, STRETCH, GROUPS, STATE)
    steps = jnp.transpose(step_size.reshape(HEADS, blocks, STRETCH), (1, 0, 2))[:, None]
    rates = jnp.transpose(decays.reshape(HEADS, blocks, STRETCH), (1, 0, 2))[:, None]
    skip = bypass_scale.reshape(GROUPS, per_group, 1)

    def advance(state, item):
        block_in, block_b, block_c, block_steps, block_rates = item
        within, block_state, accumulated_sums_list, entry = block_term_values(block_in, block_b, block_c, block_steps, block_rates)
        carried = carried_terms(block_c, state, entry)
        mamba_out = within + carried + skip * block_in.astype(jnp.float32)
        new_state = accumulated_sums_list[..., None, None] * state + block_state
        return (new_state, mamba_out[0])
    initial_state = jnp.zeros((1, GROUPS, per_group, HEADP, STATE), jnp.float32)
    final_state, outputs = lax.scan(advance, initial_state, (inputs, in_maps, out_maps, steps, rates))
    mamba_out = outputs.reshape(TOKENS, HEADS * HEADP)
    gated = mamba_out * jax.nn.silu(gate_input.astype(jnp.float32))
    grouped = gated.reshape(TOKENS, GROUPS, -1)
    factor = lax.rsqrt(lax.optimization_barrier(jnp.mean(grouped * grouped, axis=-1, keepdims=True)) + 1e-05)
    normed = ((grouped * factor).reshape(TOKENS, HEADS * HEADP) * norm_gain.astype(jnp.float32)).astype(jnp.bfloat16)
    span = HEADS * HEADP // N_HEAD
    summed = jnp.zeros((TOKENS, DOUT), jnp.float32)
    for index in range(N_HEAD):
        partial_value = jnp.dot(normed[:, index * span:(index + 1) * span], out_weight[index * span:(index + 1) * span], preferred_element_type=jnp.float32).astype(jnp.bfloat16)
        summed = summed + lax.optimization_barrier(partial_value).astype(jnp.float32)
    return summed.astype(jnp.bfloat16)
```

```python
import functools

import jax
import jax.numpy as jnp
from jax import lax
from jax.experimental import pallas as pl
from jax.experimental.pallas import tpu as pltpu
from jax.sharding import PartitionSpec as P

HEADP = 64
STATE = 256
STRETCH = 128
PIECES = 8
SPLIT = 4
LAST_SPLIT = 5
MATE_ROUND = 4
QUARTERS = 4
MESH = pl.DeviceIdType.MESH
F32 = jnp.float32
BF16 = jnp.bfloat16


def rows_of(k, size):
    return pl.ds(pl.multiple_of(k * size, size), size)


def layer(
    sizes,
    x_ref,
    gate_ref,
    bm_ref,
    cm_ref,
    step_ref,
    dec_ref,
    skip_ref,
    gain_ref,
    w_ref,
    out_ref,
    wg,
    part,
    sib,
    xbuf,
    racc,
    zbuf,
    y_ref,
    st,
    ent,
    inc,
    sbuf,
    normed,
    tall,
    expander,
    ramp_t,
    rows_r,
    lead_ref,
    full_ref,
    local_sem,
    keep_sem,
    w_recv,
    up_send,
    down_send,
    side_send,
    st_send,
    st_recv,
    t_send,
    t_recv,
    sib_send,
    sib_recv,
    x_send,
    x_recv,
    z_send,
    z_recv,
):
    lanes, ctx, peers = sizes
    tokens, width = x_ref.shape
    heads = step_ref.shape[0]
    groups = bm_ref.shape[1] // STATE
    blocks = tokens // STRETCH
    chunks, cw = wg.shape[1], wg.shape[3]
    depth = w_ref.shape[0]
    span = depth // PIECES
    share = lanes == 2 and chunks % 2 == 0
    line_chunks = chunks // 2 if share else chunks
    units = (ctx - 1) * line_chunks
    pairs, xs = ctx // 2, peers // 2
    gw = width // groups
    qw = width // QUARTERS
    owned = tokens // peers
    y, z, me = lax.axis_index("group"), lax.axis_index("ctx"), lax.axis_index("head")
    above, below = z + 1 < ctx, z > 0
    other = {"group": 1 - y} if share else None
    p, odd = lax.div(z, 2), lax.rem(z, 2)
    xi, core = lax.div(me, 2), lax.rem(me, 2)
    mate = z + 1 - 2 * odd

    barrier = pltpu.get_barrier_semaphore()

    def greet(target):
        pl.semaphore_signal(barrier, inc=1, device_id=target, device_id_type=MESH)

    met = jnp.int32(0)
    for d in (-2, -1, 1, 2):
        there = jnp.logical_and(z + d >= 0, z + d < ctx)

        @pl.when(there)
        def _():
            greet({"ctx": z + d})

        met = met + jnp.where(there, 1, 0)
    if share:
        greet(other)
    greet({"head": me + 1 - 2 * core})
    for d in range(1, xs):
        greet({"head": 2 * lax.rem(xi + d, xs) + core})
    pl.semaphore_wait(barrier, met + xs + (1 if share else 0))

    def split(pair):
        return jnp.where(pair == pairs - 1, LAST_SPLIT, SPLIT)

    def start_of(node):
        return jnp.where(lax.rem(node, 2) == 1, split(lax.div(node, 2)), 0)

    def holder(pair, r):
        return 2 * pair + jnp.where(r >= split(pair), 1, 0)

    cut = split(p)
    base = jnp.where(odd == 1, cut, 0)
    count = jnp.where(odd == 1, PIECES - cut, cut)
    mate_base = jnp.where(odd == 1, 0, cut)

    def sized(body):
        for n in sorted({SPLIT, PIECES - SPLIT, LAST_SPLIT, PIECES - LAST_SPLIT}):

            @pl.when(count == n)
            def _():
                body(n)

    def each(size, body):
        def go(i, carry):
            body(i)
            return carry

        lax.fori_loop(0, size, go, 0)

    def line_chunk(i):
        return 2 * i + y if share else i

    def up_target(r):
        near = jnp.logical_and(odd == 0, r >= cut)
        return jnp.where(near, z + 1, holder(p + 1, r)), jnp.logical_or(near, p + 1 < pairs)

    def down_target(r):
        near = jnp.logical_and(odd == 1, r < cut)
        return jnp.where(near, z - 1, holder(p - 1, r)), jnp.logical_or(near, p > 0)

    def place(j, c, r, node):
        return wg.at[j, c, rows_of(r - start_of(node), span)]

    def send(src, j, c, r, sem, node, target):
        return pltpu.make_async_remote_copy(
            src_ref=src,
            dst_ref=place(j, c, r, node),
            send_sem=sem.at[j, c, r],
            recv_sem=w_recv.at[j, c, r],
            device_id=target,
            device_id_type=MESH,
        )

    def arrived(j, c, r):
        near = {"head": me + 1 - 2 * core}
        send(place(j, c, r, z), j, c, r, up_send, z, near).wait_recv()

    def own_send(up, c, r, want, wait=False):
        node, there = up_target(r) if up else down_target(r)

        @pl.when(jnp.logical_and(there, want(node)))
        def _():
            src = w_ref.at[rows_of(r, span), rows_of(c, cw)]
            copy = send(src, z, c, r, up_send if up else down_send, node, {"ctx": node})
            if wait:
                copy.wait_send()
            else:
                copy.start()

    def own_sends(up, when_chunk, far):
        def body(n):
            i, r = lax.div(n, PIECES), lax.rem(n, PIECES)

            def want(node):
                gap = node - z if up else z - node
                return jnp.logical_and(when_chunk(i), gap == (2 if far else 1))

            own_send(up, line_chunk(i), r, want)

        each(line_chunks * PIECES, body)

    def first(i):
        return jnp.logical_or(i == 0, z == ctx - 2)

    own_sends(False, lambda i: i >= 0, False)
    own_sends(True, first, False)
    own_sends(False, lambda i: i >= 0, True)

    def rest_up():
        own_sends(True, lambda i: jnp.logical_not(first(i)), False)
        own_sends(True, lambda i: i >= 0, True)

    def local_copy(c, n):
        return pltpu.make_async_copy(
            w_ref.at[pl.ds(pl.multiple_of(base * span, span), n * span), rows_of(c, cw)],
            wg.at[z, c, pl.ds(0, n * span)],
            local_sem.at[c],
        )

    sized(lambda n: each(chunks, lambda c: local_copy(c, n).start()))

    downs = (ctx - 1 - z) * line_chunks

    def unit_of(v):
        falling = v < downs
        s = lax.div(jnp.where(falling, v, v - downs), line_chunks)
        return falling, jnp.where(falling, z + 1 + s, z - 1 - s), lax.rem(v, line_chunks)

    def service(v, lo, hi, wait=False):
        falling, j, i = unit_of(v)
        c = line_chunk(i)

        def body(k):
            r = base + k
            if not wait:
                arrived(j, c, r)
            for up in (True, False):
                node, there = up_target(r) if up else down_target(r)
                there = jnp.logical_and(there, jnp.logical_xor(falling, up))

                @pl.when(there)
                def _():
                    sem = up_send if up else down_send
                    copy = send(place(j, c, r, z), j, c, r, sem, node, {"ctx": node})
                    if wait:
                        copy.wait_send()
                    else:
                        copy.start()

            if share:
                copy = send(place(j, c, r, z), j, c, r, side_send, z, other)
                if wait:
                    copy.wait_send()
                else:
                    copy.start()

        lax.fori_loop(lo, hi, lambda k, carry: (body(k), carry)[1], 0)

    spots = lax.broadcasted_iota(jnp.int32, (heads, width), 1)
    owner = lax.broadcasted_iota(jnp.int32, (heads, width), 0)
    inside = jnp.logical_and(spots >= owner * HEADP, spots < owner * HEADP + HEADP)
    expander[...] = jnp.where(inside, 1.0, 0.0).astype(BF16)

    def spread(v, lo, size):
        high = v.astype(BF16)
        low = (v - high.astype(F32)).astype(BF16)
        e = expander[:, lo : lo + size]
        return jnp.dot(high, e, preferred_element_type=F32) + jnp.dot(
            low, e, preferred_element_type=F32
        )

    row_i = lax.broadcasted_iota(jnp.int32, (STRETCH, STRETCH), 0)
    col_i = lax.broadcasted_iota(jnp.int32, (STRETCH, STRETCH), 1)
    lower = row_i >= col_i
    nt = (((1,), (1,)), ((), ()))
    tn = (((0,), (0,)), ((), ()))

    st[...] = jnp.zeros_like(st)

    def states(k, lead):
        rows = rows_of(k, STRETCH)
        low_tri = jnp.where(lower, 1.0, 0.0).astype(F32)
        eye = jnp.where(row_i == col_i, 1.0, 0.0).astype(F32)
        logd = jnp.log(dec_ref[:, rows])
        logs = jnp.log(step_ref[:, rows])
        exact = functools.partial(
            lax.dot_general,
            dimension_numbers=nt,
            precision=lax.Precision.HIGHEST,
            preferred_element_type=F32,
        )
        ramp = exact(logd, low_tri)
        rt = exact(low_tri, logd)
        st_t = exact(eye, logs)
        rows_r[k] = ramp - logs
        ramp_t[k] = rt
        lead_ref[k] = lead
        end = rt[STRETCH - 1 : STRETCH, :]
        tails = jnp.exp(end - (rt - st_t))
        total = jnp.broadcast_to(jnp.exp(end), (8, heads))
        for g in range(groups):
            cols = slice(g * gw, (g + 1) * gw)
            weighted = (x_ref[rows, cols].astype(F32) * spread(tails, g * gw, gw)).astype(BF16)
            made = lax.dot_general(
                bm_ref[rows, g * STATE : (g + 1) * STATE],
                weighted,
                tn,
                preferred_element_type=F32,
            )
            old = st[:, cols]
            ent[k, :, cols] = old.astype(BF16)
            st[:, cols] = spread(total, g * gw, gw)[0:1] * old + made
        return lead + jnp.broadcast_to(end, (8, heads))

    lead = lax.fori_loop(0, blocks, states, jnp.zeros((8, heads), F32))
    full_ref[...] = jnp.exp(lead)

    def state_copy(q):
        return pltpu.make_async_remote_copy(
            src_ref=sbuf.at[q],
            dst_ref=inc.at[q],
            send_sem=st_send.at[q],
            recv_sem=st_recv.at[q],
            device_id={"ctx": z + 1},
            device_id_type=MESH,
        )

    @pl.when(z == 0)
    def _():
        for q in range(QUARTERS):
            inc[q] = jnp.zeros_like(inc[q])
            sbuf[q] = st[:, q * qw : (q + 1) * qw].astype(BF16)

            @pl.when(above)
            def _():
                state_copy(q).start()

    def chain():
        for q in range(QUARTERS):
            if q // 2 < units:
                service(q // 2, 0 if q % 2 == 0 else 2, 2 if q % 2 == 0 else count)
            pltpu.make_async_remote_copy(
                src_ref=sbuf.at[q],
                dst_ref=inc.at[q],
                send_sem=st_send.at[q],
                recv_sem=st_recv.at[q],
                device_id={"ctx": z - 1},
                device_id_type=MESH,
            ).wait_recv()

            @pl.when(above)
            def _():
                fall = spread(full_ref[...], q * qw, qw)[0:1]
                held = st[:, q * qw : (q + 1) * qw]
                sbuf[q] = (fall * inc[q].astype(F32) + held).astype(BF16)
                state_copy(q).start()

    half = lax.broadcasted_iota(jnp.int32, (STRETCH, 2 * HEADP), 1) < HEADP
    keep_lo = jnp.where(half, 1.0, 0.0).astype(BF16)
    keep_hi = jnp.where(half, 0.0, 1.0).astype(BF16)
    per_group = heads // groups

    def own_block(k, carry):
        rows = rows_of(k, STRETCH)
        rt = ramp_t[k]
        rr = rows_r[k]
        entry = jnp.exp(rt)
        for g in range(groups):
            c_map = cm_ref[rows, g * STATE : (g + 1) * STATE]
            b_map = bm_ref[rows, g * STATE : (g + 1) * STATE]
            scores = lax.dot_general(c_map, b_map, nt, preferred_element_type=F32)
            cols = slice(g * gw, (g + 1) * gw)
            skip = spread(jnp.broadcast_to(skip_ref[...], (8, heads)), g * gw, gw)[0:1]
            y_ref[rows, cols] = (
                jnp.dot(c_map, ent[k, :, cols], preferred_element_type=F32)
                * spread(entry, g * gw, gw)
                + skip * x_ref[rows, cols].astype(F32)
            )
            for pair in range(per_group // 2):
                mixes = []
                for h in (g * per_group + 2 * pair, g * per_group + 2 * pair + 1):
                    fade = jnp.where(lower, rt[:, h : h + 1] - rr[h : h + 1, :], -1e30)
                    mixes.append((scores * jnp.exp(fade)).astype(BF16))
                at = slice(g * gw + pair * 2 * HEADP, g * gw + (pair + 1) * 2 * HEADP)
                both = x_ref[rows, at]
                y_ref[rows, at] += jnp.dot(
                    jnp.concatenate(mixes, axis=1),
                    jnp.concatenate([both * keep_lo, both * keep_hi], axis=0),
                    preferred_element_type=F32,
                )

        return carry

    lax.fori_loop(0, blocks, own_block, 0)

    @pl.when(below)
    def _():
        chain()

    @pl.when(odd == 1)
    def _():
        rest_up()

    def finish_block(k, carry):
        rows = rows_of(k, STRETCH)
        reach = jnp.exp(ramp_t[k] + lead_ref[k, 0:1])
        squares = [jnp.zeros((STRETCH, 1), F32) for _ in range(groups)]
        for q in range(QUARTERS):
            g = q * qw // gw
            cols = slice(q * qw, (q + 1) * qw)
            carried = jnp.dot(
                cm_ref[rows, g * STATE : (g + 1) * STATE], inc[q], preferred_element_type=F32
            )
            gate = gate_ref[rows, cols].astype(F32)
            gated = (y_ref[rows, cols] + carried * spread(reach, q * qw, qw)) * (
                gate / (1.0 + jnp.exp(-gate))
            )
            y_ref[rows, cols] = gated
            squares[g] = squares[g] + jnp.sum(gated * gated, axis=1, keepdims=True)
        for g in range(groups):
            cols = slice(g * gw, (g + 1) * gw)
            factor = lax.rsqrt(squares[g] / gw + 1e-05)
            normed[rows, cols] = (y_ref[rows, cols] * factor * gain_ref[:, cols].astype(F32)).astype(
                BF16
            )

        sized(lambda n: share_block(k, n))
        return carry

    def keep_copy(k, n):
        return pltpu.make_async_copy(
            normed.at[rows_of(k, STRETCH), pl.ds(pl.multiple_of(base * span, span), n * span)],
            tall.at[0, rows_of(k, STRETCH), pl.ds(0, n * span)],
            keep_sem.at[k],
        )

    def mate_copy(k, start, n):
        return pltpu.make_async_remote_copy(
            src_ref=normed.at[
                rows_of(k, STRETCH), pl.ds(pl.multiple_of(start * span, span), n * span)
            ],
            dst_ref=tall.at[1, rows_of(k, STRETCH), pl.ds(0, n * span)],
            send_sem=t_send.at[k],
            recv_sem=t_recv.at[k],
            device_id={"ctx": mate},
            device_id_type=MESH,
        )

    def share_block(k, n):
        mate_copy(k, mate_base, PIECES - n).start()
        keep_copy(k, n).start()

    lax.fori_loop(0, blocks, finish_block, 0)
    sized(lambda n: each(blocks, lambda k: keep_copy(k, n).wait()))

    @pl.when(odd == 0)
    def _():
        rest_up()

    @pl.when(z == 0)
    def _():
        for v in range(min(2, units)):
            service(v, 0, count)

    def sib_copy(o, j, c):
        return pltpu.make_async_remote_copy(
            src_ref=part.at[o, j, c, 1 - core],
            dst_ref=sib.at[o, j, c],
            send_sem=sib_send.at[o, j, c],
            recv_sem=sib_recv.at[o, j, c],
            device_id={"head": me + 1 - 2 * core},
            device_id_type=MESH,
        )

    def x_copy(o, j, c, d):
        there = lax.rem(xi + d, xs)
        return pltpu.make_async_remote_copy(
            src_ref=part.at[o, j, c, core, there],
            dst_ref=xbuf.at[d - 1, o, j, c],
            send_sem=x_send.at[d - 1, o, j, c],
            recv_sem=x_recv.at[d - 1, o, j, c],
            device_id={"head": 2 * there + core},
            device_id_type=MESH,
        )

    def z_copy(j, c):
        return pltpu.make_async_remote_copy(
            src_ref=part.at[1, j, c, core, xi],
            dst_ref=zbuf.at[j, c],
            send_sem=z_send.at[j, c],
            recv_sem=z_recv.at[j, c],
            device_id={"ctx": mate},
            device_id_type=MESH,
        )

    def multiply(o, j, c):
        def body(n):
            made = jnp.dot(
                tall[o, :, : n * span], wg[j, c, : n * span, :], preferred_element_type=F32
            ).astype(BF16)
            for h in range(peers):
                part[o, j, c, h % 2, h // 2] = made[h * owned : (h + 1) * owned]

        sized(body)
        sib_copy(o, j, c).start()

    def decode(code):
        o, u = lax.div(code, ctx * chunks), lax.rem(code, ctx * chunks)
        return o, lax.div(u, chunks), lax.rem(u, chunks)

    def chip_sum(code):
        @pl.when(code >= 0)
        def _():
            o, j, c = decode(code)
            sib_copy(o, j, c).wait_recv()
            part[o, j, c, core] = (
                part[o, j, c, core].astype(F32) + sib[o, j, c].astype(F32)
            ).astype(BF16)
            for d in range(1, xs):
                x_copy(o, j, c, d).start()

    def head_sum(code):
        @pl.when(code >= 0)
        def _():
            o, j, c = decode(code)
            total = part[o, j, c, core, xi].astype(F32)
            for d in range(1, xs):
                x_copy(o, j, c, d).wait_recv()
                total = total + xbuf[d - 1, o, j, c].astype(F32)

            @pl.when(o == 0)
            def _():
                racc[j, c] = total

            @pl.when(o == 1)
            def _():
                part[1, j, c, core, xi] = total.astype(BF16)
                z_copy(j, c).start()

    late = min(MATE_ROUND, units)
    own_kind, line_kind, side_kind = 0, 1, 2
    items = [(0, own_kind, c, 0, 0) for c in range(chunks)]
    for v in range(units + 1):
        if v == late:
            waiting = [(own_kind, c) for c in range(chunks)]
            for w in range(late):
                waiting.append((line_kind, w))
                if share and w:
                    waiting.append((side_kind, w - 1))
            items += [(1, kind, i, 0, 1 if n == 0 else 0) for n, (kind, i) in enumerate(waiting)]
        turns = [(line_kind, v)] if v < units else []
        if share and v:
            turns.append((side_kind, v - 1))
        for n, (kind, i) in enumerate(turns):
            items.append((0, kind, i, 1 if n == 0 and 2 <= v < units else 0, 0))
            if v >= late:
                items.append((1, kind, i, 0, 0))
    size = max(units, chunks)
    table = [(((o * 3 + kind) * size + i) * 2 + svc) * 2 + hold for o, kind, i, svc, hold in items]

    def item(t, carry):
        code = jnp.int32(table[0])
        for n in range(1, len(table)):
            code = jnp.where(t == n, table[n], code)
        hold, code = lax.rem(code, 2), lax.div(code, 2)
        svc, code = lax.rem(code, 2), lax.div(code, 2)
        i, code = lax.rem(code, size), lax.div(code, size)
        kind, o = lax.rem(code, 3), lax.div(code, 3)

        @pl.when(svc == 1)
        def _():
            service(i, 0, count)

        @pl.when(hold == 1)
        def _():
            sized(lambda n: each(blocks, lambda k: mate_copy(k, base, n).wait_recv()))

        _, j, at = unit_of(i)
        own = kind == own_kind
        j = jnp.where(own, z, j)
        c = jnp.where(own, i, line_chunk(at))
        if share:
            c = jnp.where(kind == side_kind, 2 * at + 1 - y, c)

        @pl.when(jnp.logical_and(own, o == 0))
        def _():
            sized(lambda n: local_copy(c, n).wait())

        if share:

            @pl.when(jnp.logical_and(kind == side_kind, o == 0))
            def _():
                each(count, lambda k: arrived(j, c, base + k))

        multiply(o, j, c)
        chip_sum(carry[0])
        head_sum(carry[2])
        return ((o * ctx + j) * chunks + c, carry[0], carry[1])

    none = jnp.int32(-1)
    last = lax.fori_loop(0, len(table), item, (none, none, none))
    chip_sum(last[0])
    for n in (2, 1, 0):
        head_sum(last[n])

    def collect(u):
        j, c = lax.div(u, chunks), lax.rem(u, chunks)
        z_copy(j, c).wait_recv()
        out_ref[:, rows_of(u, cw)] = (racc[j, c] + zbuf[j, c].astype(F32)).astype(BF16)

    each(ctx * chunks, collect)

    def own_done(n):
        c, r = line_chunk(lax.div(n, PIECES)), lax.rem(n, PIECES)
        own_send(True, c, r, lambda node: node >= 0, True)
        own_send(False, c, r, lambda node: node >= 0, True)

    each(line_chunks * PIECES, own_done)
    each(units, lambda v: service(v, 0, count, True))

    @pl.when(above)
    def _():
        for q in range(QUARTERS):
            state_copy(q).wait_send()

    sized(lambda n: each(blocks, lambda k: mate_copy(k, mate_base, PIECES - n).wait_send()))

    def sent(u):
        j, c = lax.div(u, chunks), lax.rem(u, chunks)
        for o in range(2):
            sib_copy(o, j, c).wait_send()
            for d in range(1, xs):
                x_copy(o, j, c, d).wait_send()
        z_copy(j, c).wait_send()

    each(ctx * chunks, sent)


def shards(
    sizes,
    head_input,
    gate_input,
    input_map,
    output_map,
    step_size,
    decays,
    bypass_scale,
    norm_gain,
    out_weight,
):
    lanes, ctx, peers = sizes
    tokens, width = head_input.shape
    heads = step_size.shape[0]
    blocks = tokens // STRETCH
    depth, cols = out_weight.shape
    cw = min(cols, 256)
    chunks = cols // cw
    owned, xs = tokens // peers, peers // 2
    most = max(SPLIT, PIECES - SPLIT, LAST_SPLIT, PIECES - LAST_SPLIT)
    dma = pltpu.SemaphoreType.DMA
    vmem = pl.BlockSpec(memory_space=pltpu.VMEM)
    return pl.pallas_call(
        functools.partial(layer, sizes),
        out_shape=jax.ShapeDtypeStruct((owned, ctx * cols), BF16),
        in_specs=[vmem] * 8 + [pl.BlockSpec(memory_space=pl.ANY)],
        out_specs=vmem,
        scratch_shapes=[
            pltpu.VMEM((ctx, chunks, most * depth // PIECES, cw), BF16),
            pltpu.VMEM((2, ctx, chunks, 2, xs, owned, cw), BF16),
            pltpu.VMEM((2, ctx, chunks, xs, owned, cw), BF16),
            pltpu.VMEM((max(xs - 1, 1), 2, ctx, chunks, owned, cw), BF16),
            pltpu.VMEM((ctx, chunks, owned, cw), F32),
            pltpu.VMEM((ctx, chunks, owned, cw), BF16),
            pltpu.VMEM((tokens, width), F32),
            pltpu.VMEM((STATE, width), F32),
            pltpu.VMEM((blocks, STATE, width), BF16),
            pltpu.VMEM((QUARTERS, STATE, width // QUARTERS), BF16),
            pltpu.VMEM((QUARTERS, STATE, width // QUARTERS), BF16),
            pltpu.VMEM((tokens, width), BF16),
            pltpu.VMEM((2, tokens, most * depth // PIECES), BF16),
            pltpu.VMEM((heads, width), BF16),
            pltpu.VMEM((blocks, STRETCH, heads), F32),
            pltpu.VMEM((blocks, heads, STRETCH), F32),
            pltpu.VMEM((blocks, 8, heads), F32),
            pltpu.VMEM((8, heads), F32),
            dma((chunks,)),
            dma((blocks,)),
            dma((ctx, chunks, PIECES)),
            dma((ctx, chunks, PIECES)),
            dma((ctx, chunks, PIECES)),
            dma((ctx, chunks, PIECES)),
            dma((QUARTERS,)),
            dma((QUARTERS,)),
            dma((blocks,)),
            dma((blocks,)),
            dma((2, ctx, chunks)),
            dma((2, ctx, chunks)),
            dma((max(xs - 1, 1), 2, ctx, chunks)),
            dma((max(xs - 1, 1), 2, ctx, chunks)),
            dma((ctx, chunks)),
            dma((ctx, chunks)),
        ],
        compiler_params=pltpu.CompilerParams(
            collective_id=0, has_side_effects=True, vmem_limit_bytes=60 << 20
        ),
    )(
        head_input,
        gate_input,
        input_map,
        output_map,
        step_size,
        decays,
        bypass_scale.reshape(1, heads),
        norm_gain.reshape(1, width),
        out_weight,
    )


def solution(mesh):
    sizes = (mesh.shape["group"], mesh.shape["ctx"], mesh.shape["head"])
    return jax.shard_map(
        functools.partial(shards, sizes),
        mesh=mesh,
        in_specs=(
            P(("group", "ctx"), "head"),
            P(("group", "ctx"), "head"),
            P(("group", "ctx"), "head"),
            P(("group", "ctx"), "head"),
            P("head", ("group", "ctx")),
            P("head", ("group", "ctx")),
            P("head"),
            P("head"),
            P("head", "ctx"),
        ),
        out_specs=P(("group", "ctx", "head"), None),
        check_vma=False,
    )
```

```python
import functools

import jax
import jax.numpy as jnp
from jax import lax
from jax.experimental import pallas as pl
from jax.experimental.pallas import tpu as pltpu
from jax.sharding import PartitionSpec as P

HEADP = 64
STATE = 256
STRETCH = 128
PIECES = 8
SPLIT = 4
LAST_SPLIT = 5
MATE_ROUND = 4
QUARTERS = 8
CHIP_LAG = 2
HEAD_LAG = 7
HEAD_START = 3
MESH = pl.DeviceIdType.MESH
F32 = jnp.float32
BF16 = jnp.bfloat16


def rows_of(k, size):
    return pl.ds(pl.multiple_of(k * size, size), size)


def layer(
    sizes,
    x_any,
    gate_any,
    bm_any,
    cm_any,
    step_ref,
    dec_ref,
    skip_ref,
    gain_ref,
    w_ref,
    out_ref,
    x_ref,
    gate_ref,
    bm_ref,
    cm_ref,
    wg,
    part,
    sib,
    xbuf,
    racc,
    zbuf,
    y_ref,
    st,
    ent,
    inc,
    sbuf,
    normed,
    tall,
    expander,
    ramp_t,
    rows_r,
    lead_ref,
    full_ref,
    load_sem,
    local_sem,
    m_recv,
    w_recv,
    up_send,
    down_send,
    side_send,
    st_send,
    st_recv,
    t_send,
    t_recv,
    sib_send,
    sib_recv,
    x_send,
    x_recv,
    z_send,
    z_recv,
):
    lanes, ctx, peers = sizes
    tokens, width = x_ref.shape
    heads = step_ref.shape[0]
    groups = bm_ref.shape[1] // STATE
    blocks = tokens // STRETCH
    chunks, cw = wg.shape[1], wg.shape[3]
    depth = w_ref.shape[0]
    span = depth // PIECES
    share = lanes == 2 and chunks % 2 == 0
    line_chunks = chunks // 2 if share else chunks
    units = (ctx - 1) * line_chunks
    pairs, xs = ctx // 2, peers // 2
    gw = width // groups
    qw = width // QUARTERS
    owned = tokens // peers
    y, z, me = lax.axis_index("group"), lax.axis_index("ctx"), lax.axis_index("head")
    above, below = z + 1 < ctx, z > 0
    other = {"group": 1 - y} if share else None
    p, odd = lax.div(z, 2), lax.rem(z, 2)
    xi, core = lax.div(me, 2), lax.rem(me, 2)
    mate = z + 1 - 2 * odd

    loads = [
        pltpu.make_async_copy(src, dst, load_sem.at[n])
        for n, (src, dst) in enumerate(
            ((x_any, x_ref), (bm_any, bm_ref), (cm_any, cm_ref), (gate_any, gate_ref))
        )
    ]

    barrier = pltpu.get_barrier_semaphore()

    def greet(target):
        pl.semaphore_signal(barrier, inc=1, device_id=target, device_id_type=MESH)

    met = jnp.int32(0)
    for d in (-2, -1, 1, 2):
        there = jnp.logical_and(z + d >= 0, z + d < ctx)

        @pl.when(there)
        def _():
            greet({"ctx": z + d})

        met = met + jnp.where(there, 1, 0)
    if share:
        greet(other)
    greet({"head": me + 1 - 2 * core})
    for d in range(1, xs):
        greet({"head": 2 * lax.rem(xi + d, xs) + core})
    pl.semaphore_wait(barrier, met + xs + (1 if share else 0))

    for load in loads:
        load.start()

    def split(pair):
        return jnp.where(pair == pairs - 1, LAST_SPLIT, SPLIT)

    def start_of(node):
        return jnp.where(lax.rem(node, 2) == 1, split(lax.div(node, 2)), 0)

    def holder(pair, r):
        return 2 * pair + jnp.where(r >= split(pair), 1, 0)

    cut = split(p)
    base = jnp.where(odd == 1, cut, 0)
    count = jnp.where(odd == 1, PIECES - cut, cut)
    mate_base = jnp.where(odd == 1, 0, cut)

    def sized(body):
        for n in sorted({SPLIT, PIECES - SPLIT, LAST_SPLIT, PIECES - LAST_SPLIT}):

            @pl.when(count == n)
            def _():
                body(n)

    def each(size, body):
        def go(i, carry):
            body(i)
            return carry

        lax.fori_loop(0, size, go, 0)

    def line_chunk(i):
        return 2 * i + y if share else i

    def up_target(r):
        near = jnp.logical_and(odd == 0, r >= cut)
        return jnp.where(near, z + 1, holder(p + 1, r)), jnp.logical_or(near, p + 1 < pairs)

    def down_target(r):
        near = jnp.logical_and(odd == 1, r < cut)
        return jnp.where(near, z - 1, holder(p - 1, r)), jnp.logical_or(near, p > 0)

    def place(j, c, r, node):
        return wg.at[j, c, rows_of(r - start_of(node), span)]

    def send(src, j, c, r, sem, node, target):
        return pltpu.make_async_remote_copy(
            src_ref=src,
            dst_ref=place(j, c, r, node),
            send_sem=sem.at[j, c, r],
            recv_sem=w_recv.at[j, c, r],
            device_id=target,
            device_id_type=MESH,
        )

    def arrived(j, c, r):
        near = {"head": me + 1 - 2 * core}
        send(place(j, c, r, z), j, c, r, up_send, z, near).wait_recv()

    def own_send(up, c, r, want, wait=False):
        node, there = up_target(r) if up else down_target(r)

        @pl.when(jnp.logical_and(there, want(node)))
        def _():
            src = w_ref.at[rows_of(r, span), rows_of(c, cw)]
            copy = send(src, z, c, r, up_send if up else down_send, node, {"ctx": node})
            if wait:
                copy.wait_send()
            else:
                copy.start()

    def own_sends(up, when, far):
        def body(n):
            i, r = lax.div(n, PIECES), lax.rem(n, PIECES)
            r = r if up else PIECES - 1 - r

            def want(node):
                gap = node - z if up else z - node
                return jnp.logical_and(when(i, r), gap == (2 if far else 1))

            own_send(up, line_chunk(i), r, want)

        each(line_chunks * PIECES, body)

    def early_up(i, r):
        few = jnp.logical_and(i == 0, jnp.logical_or(z > 0, r < SPLIT + HEAD_START))
        return jnp.logical_or(few, z == ctx - 2)

    def always(i, r):
        return i >= 0

    own_sends(True, early_up, False)
    own_sends(False, always, False)
    own_sends(False, always, True)

    def rest_up():
        own_sends(True, lambda i, r: jnp.logical_not(early_up(i, r)), False)
        far_up()

    def far_up():
        own_sends(True, always, True)

    def local_copy(c, n):
        return pltpu.make_async_copy(
            w_ref.at[pl.ds(pl.multiple_of(base * span, span), n * span), rows_of(c, cw)],
            wg.at[z, c, pl.ds(0, n * span)],
            local_sem.at[c],
        )

    sized(lambda n: each(chunks, lambda c: local_copy(c, n).start()))

    over, under = ctx - 1 - z, z
    both = jnp.minimum(under, jnp.maximum(over - 1, 0))

    def unit_of(v):
        opening = jnp.logical_and(over > 0, v < line_chunks)
        w = v - jnp.where(over > 0, line_chunks, 0)
        mixed = w < 2 * line_chunks * both
        w = jnp.where(opening, 0, jnp.where(mixed, w, w - 2 * line_chunks * both))
        within = lax.rem(w, 2 * line_chunks)
        s = jnp.where(mixed, lax.div(w, 2 * line_chunks), both + lax.div(w, line_chunks)) + 1
        i = jnp.where(mixed, lax.div(within, 2), lax.rem(w, line_chunks))
        falling = jnp.where(mixed, lax.rem(within, 2) == 1, over - 1 > both)
        s = jnp.where(opening, 0, s)
        i = jnp.where(opening, v, i)
        falling = jnp.logical_or(opening, falling)
        return falling, jnp.where(falling, z + 1 + s, z - s), i

    def service(v, lo, hi, wait=False):
        falling, j, i = unit_of(v)
        c = line_chunk(i)

        def body(k):
            r = base + jnp.where(falling, count - 1 - k, k)
            if not wait:
                arrived(j, c, r)
            for up in (True, False):
                node, there = up_target(r) if up else down_target(r)
                there = jnp.logical_and(there, jnp.logical_xor(falling, up))

                @pl.when(there)
                def _():
                    sem = up_send if up else down_send
                    copy = send(place(j, c, r, z), j, c, r, sem, node, {"ctx": node})
                    if wait:
                        copy.wait_send()
                    else:
                        copy.start()

            if share:
                copy = send(place(j, c, r, z), j, c, r, side_send, z, other)
                if wait:
                    copy.wait_send()
                else:
                    copy.start()

        lax.fori_loop(lo, hi, lambda k, carry: (body(k), carry)[1], 0)

    spots = lax.broadcasted_iota(jnp.int32, (heads, width), 1)
    owner = lax.broadcasted_iota(jnp.int32, (heads, width), 0)
    inside = jnp.logical_and(spots >= owner * HEADP, spots < owner * HEADP + HEADP)
    expander[...] = jnp.where(inside, 1.0, 0.0).astype(BF16)

    def spread(v, lo, size):
        high = v.astype(BF16)
        low = (v - high.astype(F32)).astype(BF16)
        e = expander[:, lo : lo + size]
        return jnp.dot(high, e, preferred_element_type=F32) + jnp.dot(
            low, e, preferred_element_type=F32
        )

    row_i = lax.broadcasted_iota(jnp.int32, (STRETCH, STRETCH), 0)
    col_i = lax.broadcasted_iota(jnp.int32, (STRETCH, STRETCH), 1)
    lower = row_i >= col_i
    nt = (((1,), (1,)), ((), ()))
    tn = (((0,), (0,)), ((), ()))

    st[...] = jnp.zeros_like(st)

    def states(k, lead):
        rows = rows_of(k, STRETCH)
        low_tri = jnp.where(lower, 1.0, 0.0).astype(F32)
        eye = jnp.where(row_i == col_i, 1.0, 0.0).astype(F32)
        logd = jnp.log(dec_ref[:, rows])
        logs = jnp.log(step_ref[:, rows])
        exact = functools.partial(
            lax.dot_general,
            dimension_numbers=nt,
            precision=lax.Precision.HIGHEST,
            preferred_element_type=F32,
        )
        ramp = exact(logd, low_tri)
        rt = exact(low_tri, logd)
        st_t = exact(eye, logs)
        rows_r[k] = ramp - logs
        ramp_t[k] = rt
        lead_ref[k] = lead
        end = rt[STRETCH - 1 : STRETCH, :]
        tails = jnp.exp(end - (rt - st_t))
        total = jnp.broadcast_to(jnp.exp(end), (8, heads))
        for g in range(groups):
            cols = slice(g * gw, (g + 1) * gw)
            weighted = (x_ref[rows, cols].astype(F32) * spread(tails, g * gw, gw)).astype(BF16)
            made = lax.dot_general(
                bm_ref[rows, g * STATE : (g + 1) * STATE],
                weighted,
                tn,
                preferred_element_type=F32,
            )
            old = st[:, cols]
            ent[k, :, cols] = old.astype(BF16)
            st[:, cols] = spread(total, g * gw, gw)[0:1] * old + made
        return lead + jnp.broadcast_to(end, (8, heads))

    loads[0].wait()
    loads[1].wait()
    lead = lax.fori_loop(0, blocks, states, jnp.zeros((8, heads), F32))
    full_ref[...] = jnp.exp(lead)

    def state_copy(q):
        return pltpu.make_async_remote_copy(
            src_ref=sbuf.at[q],
            dst_ref=inc.at[q],
            send_sem=st_send.at[q],
            recv_sem=st_recv.at[q],
            device_id={"ctx": z + 1},
            device_id_type=MESH,
        )

    @pl.when(z == 0)
    def _():
        for q in range(QUARTERS):
            inc[q] = jnp.zeros_like(inc[q])
            sbuf[q] = st[:, q * qw : (q + 1) * qw].astype(BF16)

            @pl.when(above)
            def _():
                state_copy(q).start()

        own_sends(True, lambda i, r: jnp.logical_not(early_up(i, r)), False)

    early = min(2, units)
    stage = QUARTERS // 2

    def chain(q):
        if q // stage < early:
            at = q % stage
            service(q // stage, at, count if at == stage - 1 else jnp.minimum(at + 1, count))
        pltpu.make_async_remote_copy(
            src_ref=sbuf.at[q],
            dst_ref=inc.at[q],
            send_sem=st_send.at[q],
            recv_sem=st_recv.at[q],
            device_id={"ctx": z - 1},
            device_id_type=MESH,
        ).wait_recv()

        @pl.when(above)
        def _():
            fall = spread(full_ref[...], q * qw, qw)[0:1]
            held = st[:, q * qw : (q + 1) * qw]
            sbuf[q] = (fall * inc[q].astype(F32) + held).astype(BF16)
            state_copy(q).start()

    half = lax.broadcasted_iota(jnp.int32, (STRETCH, 2 * HEADP), 1) < HEADP
    keep_lo = jnp.where(half, 1.0, 0.0).astype(BF16)
    keep_hi = jnp.where(half, 0.0, 1.0).astype(BF16)
    per_group = heads // groups

    def own_block(k, carry):
        rows = rows_of(k, STRETCH)
        rt = ramp_t[k]
        rr = rows_r[k]
        entry = jnp.exp(rt)
        for g in range(groups):
            c_map = cm_ref[rows, g * STATE : (g + 1) * STATE]
            b_map = bm_ref[rows, g * STATE : (g + 1) * STATE]
            scores = lax.dot_general(c_map, b_map, nt, preferred_element_type=F32)
            cols = slice(g * gw, (g + 1) * gw)
            skip = spread(jnp.broadcast_to(skip_ref[...], (8, heads)), g * gw, gw)[0:1]
            y_ref[rows, cols] = (
                jnp.dot(c_map, ent[k, :, cols], preferred_element_type=F32)
                * spread(entry, g * gw, gw)
                + skip * x_ref[rows, cols].astype(F32)
            )
            for pair in range(per_group // 2):
                mixes = []
                for h in (g * per_group + 2 * pair, g * per_group + 2 * pair + 1):
                    fade = jnp.where(lower, rt[:, h : h + 1] - rr[h : h + 1, :], -1e30)
                    mixes.append((scores * jnp.exp(fade)).astype(BF16))
                at = slice(g * gw + pair * 2 * HEADP, g * gw + (pair + 1) * 2 * HEADP)
                both = x_ref[rows, at]
                y_ref[rows, at] += jnp.dot(
                    jnp.concatenate(mixes, axis=1),
                    jnp.concatenate([both * keep_lo, both * keep_hi], axis=0),
                    preferred_element_type=F32,
                )

        return carry

    loads[2].wait()
    lax.fori_loop(0, blocks, own_block, 0)
    loads[3].wait()

    def finish_group(g, k):
        rows = rows_of(k, STRETCH)
        reach = jnp.exp(ramp_t[k] + lead_ref[k, 0:1])
        squares = jnp.zeros((STRETCH, 1), F32)
        for q in range(g * gw // qw, (g + 1) * gw // qw):
            cols = slice(q * qw, (q + 1) * qw)
            carried = jnp.dot(
                cm_ref[rows, g * STATE : (g + 1) * STATE], inc[q], preferred_element_type=F32
            )
            gate = gate_ref[rows, cols].astype(F32)
            gated = (y_ref[rows, cols] + carried * spread(reach, q * qw, qw)) * (
                gate / (1.0 + jnp.exp(-gate))
            )
            y_ref[rows, cols] = gated
            squares = squares + jnp.sum(gated * gated, axis=1, keepdims=True)
        cols = slice(g * gw, (g + 1) * gw)
        factor = lax.rsqrt(squares / gw + 1e-05)
        normed[rows, cols] = (y_ref[rows, cols] * factor * gain_ref[:, cols].astype(F32)).astype(
            BF16
        )

    def keep_copy(r):
        return pltpu.make_async_copy(
            normed.at[:, rows_of(r, span)], tall.at[0, :, rows_of(r - base, span)], t_recv.at[r]
        )

    def mate_copy(r, start):
        return pltpu.make_async_remote_copy(
            src_ref=normed.at[:, rows_of(r, span)],
            dst_ref=tall.at[1, :, rows_of(r - start, span)],
            send_sem=t_send.at[r],
            recv_sem=m_recv.at[r],
            device_id={"ctx": mate},
            device_id_type=MESH,
        )

    def share_piece(r):
        mine = jnp.logical_and(r >= base, r < base + count)

        @pl.when(mine)
        def _():
            keep_copy(r).start()

        @pl.when(jnp.logical_not(mine))
        def _():
            mate_copy(r, mate_base).start()

    for g in range(groups):

        @pl.when(below)
        def _():
            for q in range(g * gw // qw, (g + 1) * gw // qw):
                chain(q)

        if g == groups - 1:

            @pl.when(odd == 1)
            def _():
                rest_up()

        each(blocks, lambda k: finish_group(g, k))
        lax.fori_loop(
            g * PIECES // groups,
            (g + 1) * PIECES // groups,
            lambda r, carry: (share_piece(r), carry)[1],
            0,
        )

    @pl.when(jnp.logical_and(odd == 0, z > 0))
    def _():
        rest_up()

    @pl.when(z == 0)
    def _():
        far_up()

    each(count, lambda k: keep_copy(base + k).wait())

    @pl.when(z == 0)
    def _():
        for v in range(early):
            service(v, 0, count)

    def sib_copy(o, j, c):
        return pltpu.make_async_remote_copy(
            src_ref=part.at[o, j, c, 1 - core],
            dst_ref=sib.at[o, j, c],
            send_sem=sib_send.at[o, j, c],
            recv_sem=sib_recv.at[o, j, c],
            device_id={"head": me + 1 - 2 * core},
            device_id_type=MESH,
        )

    def x_copy(o, j, c, d):
        there = lax.rem(xi + d, xs)
        return pltpu.make_async_remote_copy(
            src_ref=part.at[o, j, c, core, there],
            dst_ref=xbuf.at[d - 1, o, j, c],
            send_sem=x_send.at[d - 1, o, j, c],
            recv_sem=x_recv.at[d - 1, o, j, c],
            device_id={"head": 2 * there + core},
            device_id_type=MESH,
        )

    def z_copy(j, c):
        return pltpu.make_async_remote_copy(
            src_ref=part.at[1, j, c, core, xi],
            dst_ref=zbuf.at[j, c],
            send_sem=z_send.at[j, c],
            recv_sem=z_recv.at[j, c],
            device_id={"ctx": mate},
            device_id_type=MESH,
        )

    def multiply(o, j, c):
        def body(n):
            made = jnp.dot(
                tall[o, :, : n * span], wg[j, c, : n * span, :], preferred_element_type=F32
            ).astype(BF16)
            for h in range(peers):
                part[o, j, c, h % 2, h // 2] = made[h * owned : (h + 1) * owned]

        sized(body)
        sib_copy(o, j, c).start()

    def decode(code):
        o, u = lax.div(code, ctx * chunks), lax.rem(code, ctx * chunks)
        return o, lax.div(u, chunks), lax.rem(u, chunks)

    def chip_sum(code):
        @pl.when(code >= 0)
        def _():
            o, j, c = decode(code)
            sib_copy(o, j, c).wait_recv()
            part[o, j, c, core] = (
                part[o, j, c, core].astype(F32) + sib[o, j, c].astype(F32)
            ).astype(BF16)
            for d in range(1, xs):
                x_copy(o, j, c, d).start()

    def head_sum(code):
        @pl.when(code >= 0)
        def _():
            o, j, c = decode(code)
            sib_copy(o, j, c).wait_send()
            total = part[o, j, c, core, xi].astype(F32)
            for d in range(1, xs):
                x_copy(o, j, c, d).wait()
                total = total + xbuf[d - 1, o, j, c].astype(F32)

            @pl.when(o == 0)
            def _():
                racc[j, c] = total

            @pl.when(o == 1)
            def _():
                part[1, j, c, core, xi] = total.astype(BF16)
                z_copy(j, c).start()

    late = min(MATE_ROUND, units)
    own_kind, line_kind, side_kind = 0, 1, 2
    items = [(0, own_kind, c, 1, 0, 0) for c in range(chunks)]
    for v in range(units + 1):
        if v == late:
            waiting = [(own_kind, c) for c in range(chunks)]
            for w in range(late):
                waiting.append((line_kind, w))
                if share and w:
                    waiting.append((side_kind, w - 1))
            items += [(1, kind, i, 0, 0, int(n == 0)) for n, (kind, i) in enumerate(waiting)]
        turns = [(line_kind, v)] if v < units else []
        if share and v:
            turns.append((side_kind, v - 1))
        for n, (kind, i) in enumerate(turns):
            svc = int(n == 0 and early <= v < units)
            if v >= late:
                items += [(1, kind, i, 1, svc, 0), (0, kind, i, 0, 0, 0)]
            else:
                items.append((0, kind, i, 1, svc, 0))
    size = max(units, chunks)
    table = [
        ((((o * 3 + kind) * size + i) * 2 + new) * 2 + svc) * 2 + hold
        for o, kind, i, new, svc, hold in items
    ]
    closing = [(kind, i) for _, kind, i, *_ in items[-HEAD_LAG:]]
    settled = 0 if any(kind == own_kind for kind, _ in closing) else min(i for _, i in closing)

    def own_done(n):
        c, r = line_chunk(lax.div(n, PIECES)), lax.rem(n, PIECES)
        own_send(True, c, r, lambda node: node >= 0, True)
        own_send(False, c, r, lambda node: node >= 0, True)

    def item(t, carry):
        code = jnp.int32(table[0])
        for n in range(1, len(table)):
            code = jnp.where(t == n, table[n], code)
        hold, code = lax.rem(code, 2), lax.div(code, 2)
        svc, code = lax.rem(code, 2), lax.div(code, 2)
        new, code = lax.rem(code, 2), lax.div(code, 2)
        i, code = lax.rem(code, size), lax.div(code, size)
        kind, o = lax.rem(code, 3), lax.div(code, 3)

        @pl.when(svc == 1)
        def _():
            @pl.when(i == units - 1)
            def _():
                each(line_chunks * PIECES, own_done)
                each(settled, lambda v: service(v, 0, count, True))

            service(i, 0, count)

        @pl.when(hold == 1)
        def _():
            each(count, lambda k: mate_copy(base + k, base).wait_recv())

        _, j, at = unit_of(i)
        own = kind == own_kind
        j = jnp.where(own, z, j)
        c = jnp.where(own, i, line_chunk(at))
        if share:
            c = jnp.where(kind == side_kind, 2 * at + 1 - y, c)

        @pl.when(jnp.logical_and(own, new == 1))
        def _():
            sized(lambda n: local_copy(c, n).wait())

        if share:

            @pl.when(jnp.logical_and(kind == side_kind, new == 1))
            def _():
                each(count, lambda k: arrived(j, c, base + k))

        multiply(o, j, c)
        chip_sum(carry[CHIP_LAG - 1])
        head_sum(carry[HEAD_LAG - 1])
        return ((o * ctx + j) * chunks + c, *carry[:-1])

    none = jnp.int32(-1)
    last = lax.fori_loop(0, len(table), item, (none,) * HEAD_LAG)
    for n in range(CHIP_LAG - 1, -1, -1):
        chip_sum(last[n])

    def collect(u):
        j, c = lax.div(u, chunks), lax.rem(u, chunks)
        z_copy(j, c).wait()
        out_ref[:, rows_of(u, cw)] = (racc[j, c] + zbuf[j, c].astype(F32)).astype(BF16)

    def collect_unit(v):
        _, j, at = unit_of(v)
        collect(j * chunks + line_chunk(at))
        if share:
            collect(j * chunks + 2 * at + 1 - y)

    opened = min(line_chunks, settled)

    def collect_own(when):
        @pl.when(when)
        def _():
            each(chunks, lambda c: collect(z * chunks + c))

    if opened:
        collect_own(odd == 1)
        each(opened, collect_unit)
    for n in range(HEAD_LAG - 1, -1, -1):
        head_sum(last[n])
    each(PIECES - count, lambda k: mate_copy(mate_base + k, mate_base).wait_send())
    if units - 1 < early:
        each(line_chunks * PIECES, own_done)
        each(settled, lambda v: service(v, 0, count, True))
    lax.fori_loop(settled, units, lambda v, carry: (service(v, 0, count, True), carry)[1], 0)

    @pl.when(above)
    def _():
        for q in range(QUARTERS):
            state_copy(q).wait_send()

    collect_own(odd == 0 if opened else odd >= 0)
    lax.fori_loop(opened, units, lambda v, carry: (collect_unit(v), carry)[1], 0)


def shards(
    sizes,
    head_input,
    gate_input,
    input_map,
    output_map,
    step_size,
    decays,
    bypass_scale,
    norm_gain,
    out_weight,
):
    lanes, ctx, peers = sizes
    tokens, width = head_input.shape
    heads = step_size.shape[0]
    blocks = tokens // STRETCH
    depth, cols = out_weight.shape
    cw = min(cols, 256)
    chunks = cols // cw
    owned, xs = tokens // peers, peers // 2
    most = max(SPLIT, PIECES - SPLIT, LAST_SPLIT, PIECES - LAST_SPLIT)
    dma = pltpu.SemaphoreType.DMA
    vmem = pl.BlockSpec(memory_space=pltpu.VMEM)
    anywhere = pl.BlockSpec(memory_space=pl.ANY)
    return pl.pallas_call(
        functools.partial(layer, sizes),
        out_shape=jax.ShapeDtypeStruct((owned, ctx * cols), BF16),
        in_specs=[anywhere] * 4 + [vmem] * 4 + [anywhere],
        out_specs=vmem,
        scratch_shapes=[
            pltpu.VMEM(head_input.shape, BF16),
            pltpu.VMEM(gate_input.shape, BF16),
            pltpu.VMEM(input_map.shape, BF16),
            pltpu.VMEM(output_map.shape, BF16),
            pltpu.VMEM((ctx, chunks, most * depth // PIECES, cw), BF16),
            pltpu.VMEM((2, ctx, chunks, 2, xs, owned, cw), BF16),
            pltpu.VMEM((2, ctx, chunks, xs, owned, cw), BF16),
            pltpu.VMEM((max(xs - 1, 1), 2, ctx, chunks, owned, cw), BF16),
            pltpu.VMEM((ctx, chunks, owned, cw), F32),
            pltpu.VMEM((ctx, chunks, owned, cw), BF16),
            pltpu.VMEM((tokens, width), F32),
            pltpu.VMEM((STATE, width), F32),
            pltpu.VMEM((blocks, STATE, width), BF16),
            pltpu.VMEM((QUARTERS, STATE, width // QUARTERS), BF16),
            pltpu.VMEM((QUARTERS, STATE, width // QUARTERS), BF16),
            pltpu.VMEM((tokens, width), BF16),
            pltpu.VMEM((2, tokens, most * depth // PIECES), BF16),
            pltpu.VMEM((heads, width), BF16),
            pltpu.VMEM((blocks, STRETCH, heads), F32),
            pltpu.VMEM((blocks, heads, STRETCH), F32),
            pltpu.VMEM((blocks, 8, heads), F32),
            pltpu.VMEM((8, heads), F32),
            dma((4,)),
            dma((chunks,)),
            dma((PIECES,)),
            dma((ctx, chunks, PIECES)),
            dma((ctx, chunks, PIECES)),
            dma((ctx, chunks, PIECES)),
            dma((ctx, chunks, PIECES)),
            dma((QUARTERS,)),
            dma((QUARTERS,)),
            dma((PIECES,)),
            dma((PIECES,)),
            dma((2, ctx, chunks)),
            dma((2, ctx, chunks)),
            dma((max(xs - 1, 1), 2, ctx, chunks)),
            dma((max(xs - 1, 1), 2, ctx, chunks)),
            dma((ctx, chunks)),
            dma((ctx, chunks)),
        ],
        compiler_params=pltpu.CompilerParams(
            collective_id=0, has_side_effects=True, vmem_limit_bytes=60 << 20
        ),
    )(
        head_input,
        gate_input,
        input_map,
        output_map,
        step_size,
        decays,
        bypass_scale.reshape(1, heads),
        norm_gain.reshape(1, width),
        out_weight,
    )


def solution(mesh):
    sizes = (mesh.shape["group"], mesh.shape["ctx"], mesh.shape["head"])
    return jax.shard_map(
        functools.partial(shards, sizes),
        mesh=mesh,
        in_specs=(
            P(("group", "ctx"), "head"),
            P(("group", "ctx"), "head"),
            P(("group", "ctx"), "head"),
            P(("group", "ctx"), "head"),
            P("head", ("group", "ctx")),
            P("head", ("group", "ctx")),
            P("head"),
            P("head"),
            P("head", "ctx"),
        ),
        out_specs=P(("group", "ctx", "head"), None),
        check_vma=False,
    )
```

```python
import functools

import jax
import jax.numpy as jnp
from jax import lax
from jax.experimental import pallas as pl
from jax.experimental.pallas import tpu as pltpu
from jax.sharding import PartitionSpec as P

HEADP = 64
STATE = 256
STRETCH = 128
PIECES = 8
SPLIT = 3
LAST_SPLIT = 5
MATE_ROUND = 4
QUARTERS = 8
CHIP_LAG = 2
HEAD_LAG = 7
HEAD_START = 3
MESH = pl.DeviceIdType.MESH
F32 = jnp.float32
BF16 = jnp.bfloat16


def rows_of(k, size):
    return pl.ds(pl.multiple_of(k * size, size), size)


def layer(
    sizes,
    x_any,
    gate_any,
    bm_any,
    cm_any,
    step_ref,
    dec_ref,
    skip_ref,
    gain_ref,
    w_ref,
    out_ref,
    x_ref,
    gate_ref,
    bm_ref,
    cm_ref,
    wg,
    part,
    sib,
    xbuf,
    racc,
    zbuf,
    y_ref,
    st,
    ent,
    inc,
    sbuf,
    normed,
    tall,
    expander,
    ramp_t,
    rows_r,
    lead_ref,
    full_ref,
    load_sem,
    local_sem,
    m_recv,
    w_recv,
    up_send,
    down_send,
    side_send,
    st_send,
    st_recv,
    t_send,
    t_recv,
    sib_send,
    sib_recv,
    x_send,
    x_recv,
    z_send,
    z_recv,
):
    lanes, ctx, peers = sizes
    tokens, width = x_ref.shape
    heads = step_ref.shape[0]
    groups = bm_ref.shape[1] // STATE
    blocks = tokens // STRETCH
    chunks, cw = wg.shape[1], wg.shape[3]
    depth = w_ref.shape[0]
    span = depth // PIECES
    share = lanes == 2 and chunks % 2 == 0
    line_chunks = chunks // 2 if share else chunks
    units = (ctx - 1) * line_chunks
    pairs, xs = ctx // 2, peers // 2
    gw = width // groups
    qw = width // QUARTERS
    owned = tokens // peers
    y, z, me = lax.axis_index("group"), lax.axis_index("ctx"), lax.axis_index("head")
    above, below = z + 1 < ctx, z > 0
    other = {"group": 1 - y} if share else None
    p, odd = lax.div(z, 2), lax.rem(z, 2)
    xi, core = lax.div(me, 2), lax.rem(me, 2)
    mate = z + 1 - 2 * odd

    loads = [
        pltpu.make_async_copy(src, dst, load_sem.at[n])
        for n, (src, dst) in enumerate(
            ((x_any, x_ref), (bm_any, bm_ref), (cm_any, cm_ref), (gate_any, gate_ref))
        )
    ]

    barrier = pltpu.get_barrier_semaphore()

    def greet(target):
        pl.semaphore_signal(barrier, inc=1, device_id=target, device_id_type=MESH)

    met = jnp.int32(0)
    for d in (-2, -1, 1, 2):
        there = jnp.logical_and(z + d >= 0, z + d < ctx)

        @pl.when(there)
        def _():
            greet({"ctx": z + d})

        met = met + jnp.where(there, 1, 0)
    if share:
        greet(other)
    greet({"head": me + 1 - 2 * core})
    for d in range(1, xs):
        greet({"head": 2 * lax.rem(xi + d, xs) + core})
    pl.semaphore_wait(barrier, met + xs + (1 if share else 0))

    for load in loads:
        load.start()

    def split(pair):
        return jnp.where(pair == pairs - 1, LAST_SPLIT, SPLIT)

    def start_of(node):
        return jnp.where(lax.rem(node, 2) == 1, split(lax.div(node, 2)), 0)

    def holder(pair, r):
        return 2 * pair + jnp.where(r >= split(pair), 1, 0)

    cut = split(p)
    base = jnp.where(odd == 1, cut, 0)
    count = jnp.where(odd == 1, PIECES - cut, cut)
    mate_base = jnp.where(odd == 1, 0, cut)

    def sized(body):
        for n in sorted({SPLIT, PIECES - SPLIT, LAST_SPLIT, PIECES - LAST_SPLIT}):

            @pl.when(count == n)
            def _():
                body(n)

    def each(size, body):
        def go(i, carry):
            body(i)
            return carry

        lax.fori_loop(0, size, go, 0)

    def line_chunk(i):
        return 2 * i + y if share else i

    def up_target(r):
        near = jnp.logical_and(odd == 0, r >= cut)
        return jnp.where(near, z + 1, holder(p + 1, r)), jnp.logical_or(near, p + 1 < pairs)

    def down_target(r):
        near = jnp.logical_and(odd == 1, r < cut)
        return jnp.where(near, z - 1, holder(p - 1, r)), jnp.logical_or(near, p > 0)

    def place(j, c, r, node):
        return wg.at[j, c, rows_of(r - start_of(node), span)]

    def send(src, j, c, r, sem, node, target):
        return pltpu.make_async_remote_copy(
            src_ref=src,
            dst_ref=place(j, c, r, node),
            send_sem=sem.at[j, c, r],
            recv_sem=w_recv.at[j, c, r],
            device_id=target,
            device_id_type=MESH,
        )

    def arrived(j, c, r):
        near = {"head": me + 1 - 2 * core}
        send(place(j, c, r, z), j, c, r, up_send, z, near).wait_recv()

    def own_send(up, c, r, want, wait=False):
        node, there = up_target(r) if up else down_target(r)

        @pl.when(jnp.logical_and(there, want(node)))
        def _():
            src = w_ref.at[rows_of(r, span), rows_of(c, cw)]
            copy = send(src, z, c, r, up_send if up else down_send, node, {"ctx": node})
            if wait:
                copy.wait_send()
            else:
                copy.start()

    def own_sends(up, when, far):
        def body(n):
            i, r = lax.div(n, PIECES), lax.rem(n, PIECES)
            r = r if up else PIECES - 1 - r

            def want(node):
                gap = node - z if up else z - node
                return jnp.logical_and(when(i, r), gap == (2 if far else 1))

            own_send(up, line_chunk(i), r, want)

        each(line_chunks * PIECES, body)

    def early_up(i, r):
        few = jnp.logical_and(i == 0, jnp.logical_or(z > 0, r < SPLIT + HEAD_START))
        return jnp.logical_or(few, z == ctx - 2)

    def always(i, r):
        return i >= 0

    own_sends(True, early_up, False)
    own_sends(False, always, False)
    own_sends(False, always, True)

    def rest_up():
        own_sends(True, lambda i, r: jnp.logical_not(early_up(i, r)), False)
        far_up()

    def far_up():
        own_sends(True, always, True)

    def local_copy(c, n):
        return pltpu.make_async_copy(
            w_ref.at[pl.ds(pl.multiple_of(base * span, span), n * span), rows_of(c, cw)],
            wg.at[z, c, pl.ds(0, n * span)],
            local_sem.at[c],
        )

    sized(lambda n: each(chunks, lambda c: local_copy(c, n).start()))

    over, under = ctx - 1 - z, z
    both = jnp.minimum(under, jnp.maximum(over - 1, 0))

    def unit_of(v):
        opening = jnp.logical_and(over > 0, v < line_chunks)
        w = v - jnp.where(over > 0, line_chunks, 0)
        mixed = w < 2 * line_chunks * both
        w = jnp.where(opening, 0, jnp.where(mixed, w, w - 2 * line_chunks * both))
        within = lax.rem(w, 2 * line_chunks)
        s = jnp.where(mixed, lax.div(w, 2 * line_chunks), both + lax.div(w, line_chunks)) + 1
        i = jnp.where(mixed, lax.div(within, 2), lax.rem(w, line_chunks))
        falling = jnp.where(mixed, lax.rem(within, 2) == 1, over - 1 > both)
        s = jnp.where(opening, 0, s)
        i = jnp.where(opening, v, i)
        falling = jnp.logical_or(opening, falling)
        return falling, jnp.where(falling, z + 1 + s, z - s), i

    def service(v, lo, hi, wait=False):
        falling, j, i = unit_of(v)
        c = line_chunk(i)

        def body(k):
            r = base + jnp.where(falling, count - 1 - k, k)
            if not wait:
                arrived(j, c, r)
            for up in (True, False):
                node, there = up_target(r) if up else down_target(r)
                there = jnp.logical_and(there, jnp.logical_xor(falling, up))

                @pl.when(there)
                def _():
                    sem = up_send if up else down_send
                    copy = send(place(j, c, r, z), j, c, r, sem, node, {"ctx": node})
                    if wait:
                        copy.wait_send()
                    else:
                        copy.start()

            if share:
                copy = send(place(j, c, r, z), j, c, r, side_send, z, other)
                if wait:
                    copy.wait_send()
                else:
                    copy.start()

        lax.fori_loop(lo, hi, lambda k, carry: (body(k), carry)[1], 0)

    spots = lax.broadcasted_iota(jnp.int32, (heads, width), 1)
    owner = lax.broadcasted_iota(jnp.int32, (heads, width), 0)
    inside = jnp.logical_and(spots >= owner * HEADP, spots < owner * HEADP + HEADP)
    expander[...] = jnp.where(inside, 1.0, 0.0).astype(BF16)

    def spread(v, lo, size):
        high = v.astype(BF16)
        low = (v - high.astype(F32)).astype(BF16)
        e = expander[:, lo : lo + size]
        return jnp.dot(high, e, preferred_element_type=F32) + jnp.dot(
            low, e, preferred_element_type=F32
        )

    row_i = lax.broadcasted_iota(jnp.int32, (STRETCH, STRETCH), 0)
    col_i = lax.broadcasted_iota(jnp.int32, (STRETCH, STRETCH), 1)
    lower = row_i >= col_i
    nt = (((1,), (1,)), ((), ()))
    tn = (((0,), (0,)), ((), ()))

    st[...] = jnp.zeros_like(st)

    def states(k, lead):
        rows = rows_of(k, STRETCH)
        low_tri = jnp.where(lower, 1.0, 0.0).astype(F32)
        eye = jnp.where(row_i == col_i, 1.0, 0.0).astype(F32)
        logd = jnp.log(dec_ref[:, rows])
        logs = jnp.log(step_ref[:, rows])
        exact = functools.partial(
            lax.dot_general,
            dimension_numbers=nt,
            precision=lax.Precision.HIGHEST,
            preferred_element_type=F32,
        )
        ramp = exact(logd, low_tri)
        rt = exact(low_tri, logd)
        st_t = exact(eye, logs)
        rows_r[k] = ramp - logs
        ramp_t[k] = rt
        lead_ref[k] = lead
        end = rt[STRETCH - 1 : STRETCH, :]
        tails = jnp.exp(end - (rt - st_t))
        total = jnp.broadcast_to(jnp.exp(end), (8, heads))
        for g in range(groups):
            cols = slice(g * gw, (g + 1) * gw)
            weighted = (x_ref[rows, cols].astype(F32) * spread(tails, g * gw, gw)).astype(BF16)
            made = lax.dot_general(
                bm_ref[rows, g * STATE : (g + 1) * STATE],
                weighted,
                tn,
                preferred_element_type=F32,
            )
            old = st[:, cols]
            ent[k, :, cols] = old.astype(BF16)
            st[:, cols] = spread(total, g * gw, gw)[0:1] * old + made
        return lead + jnp.broadcast_to(end, (8, heads))

    loads[0].wait()
    loads[1].wait()
    lead = lax.fori_loop(0, blocks, states, jnp.zeros((8, heads), F32))
    full_ref[...] = jnp.exp(lead)

    def state_copy(q):
        return pltpu.make_async_remote_copy(
            src_ref=sbuf.at[q],
            dst_ref=inc.at[q],
            send_sem=st_send.at[q],
            recv_sem=st_recv.at[q],
            device_id={"ctx": z + 1},
            device_id_type=MESH,
        )

    @pl.when(z == 0)
    def _():
        for q in range(QUARTERS):
            inc[q] = jnp.zeros_like(inc[q])
            sbuf[q] = st[:, q * qw : (q + 1) * qw].astype(BF16)

            @pl.when(above)
            def _():
                state_copy(q).start()

        own_sends(True, lambda i, r: jnp.logical_not(early_up(i, r)), False)

    early = min(2, units)
    stage = QUARTERS // 2

    def chain(q):
        if q // stage < early:
            at = q % stage
            service(q // stage, at, count if at == stage - 1 else jnp.minimum(at + 1, count))
        pltpu.make_async_remote_copy(
            src_ref=sbuf.at[q],
            dst_ref=inc.at[q],
            send_sem=st_send.at[q],
            recv_sem=st_recv.at[q],
            device_id={"ctx": z - 1},
            device_id_type=MESH,
        ).wait_recv()

        @pl.when(above)
        def _():
            fall = spread(full_ref[...], q * qw, qw)[0:1]
            held = st[:, q * qw : (q + 1) * qw]
            sbuf[q] = (fall * inc[q].astype(F32) + held).astype(BF16)
            state_copy(q).start()

    half = lax.broadcasted_iota(jnp.int32, (STRETCH, 2 * HEADP), 1) < HEADP
    keep_lo = jnp.where(half, 1.0, 0.0).astype(BF16)
    keep_hi = jnp.where(half, 0.0, 1.0).astype(BF16)
    per_group = heads // groups

    def own_block(k, carry):
        rows = rows_of(k, STRETCH)
        rt = ramp_t[k]
        rr = rows_r[k]
        entry = jnp.exp(rt)
        for g in range(groups):
            c_map = cm_ref[rows, g * STATE : (g + 1) * STATE]
            b_map = bm_ref[rows, g * STATE : (g + 1) * STATE]
            scores = lax.dot_general(c_map, b_map, nt, preferred_element_type=F32)
            cols = slice(g * gw, (g + 1) * gw)
            skip = spread(jnp.broadcast_to(skip_ref[...], (8, heads)), g * gw, gw)[0:1]
            y_ref[rows, cols] = (
                jnp.dot(c_map, ent[k, :, cols], preferred_element_type=F32)
                * spread(entry, g * gw, gw)
                + skip * x_ref[rows, cols].astype(F32)
            )
            for pair in range(per_group // 2):
                mixes = []
                for h in (g * per_group + 2 * pair, g * per_group + 2 * pair + 1):
                    fade = jnp.where(lower, rt[:, h : h + 1] - rr[h : h + 1, :], -1e30)
                    mixes.append((scores * jnp.exp(fade)).astype(BF16))
                at = slice(g * gw + pair * 2 * HEADP, g * gw + (pair + 1) * 2 * HEADP)
                both = x_ref[rows, at]
                y_ref[rows, at] += jnp.dot(
                    jnp.concatenate(mixes, axis=1),
                    jnp.concatenate([both * keep_lo, both * keep_hi], axis=0),
                    preferred_element_type=F32,
                )

        return carry

    loads[2].wait()
    lax.fori_loop(0, blocks, own_block, 0)
    loads[3].wait()

    def finish_group(g, k):
        rows = rows_of(k, STRETCH)
        reach = jnp.exp(ramp_t[k] + lead_ref[k, 0:1])
        squares = jnp.zeros((STRETCH, 1), F32)
        for q in range(g * gw // qw, (g + 1) * gw // qw):
            cols = slice(q * qw, (q + 1) * qw)
            carried = jnp.dot(
                cm_ref[rows, g * STATE : (g + 1) * STATE], inc[q], preferred_element_type=F32
            )
            gate = gate_ref[rows, cols].astype(F32)
            gated = (y_ref[rows, cols] + carried * spread(reach, q * qw, qw)) * (
                gate / (1.0 + jnp.exp(-gate))
            )
            y_ref[rows, cols] = gated
            squares = squares + jnp.sum(gated * gated, axis=1, keepdims=True)
        cols = slice(g * gw, (g + 1) * gw)
        factor = lax.rsqrt(squares / gw + 1e-05)
        normed[rows, cols] = (y_ref[rows, cols] * factor * gain_ref[:, cols].astype(F32)).astype(
            BF16
        )

    def keep_copy(r):
        return pltpu.make_async_copy(
            normed.at[:, rows_of(r, span)], tall.at[0, :, rows_of(r - base, span)], t_recv.at[r]
        )

    def mate_copy(r, start):
        return pltpu.make_async_remote_copy(
            src_ref=normed.at[:, rows_of(r, span)],
            dst_ref=tall.at[1, :, rows_of(r - start, span)],
            send_sem=t_send.at[r],
            recv_sem=m_recv.at[r],
            device_id={"ctx": mate},
            device_id_type=MESH,
        )

    def share_piece(r):
        mine = jnp.logical_and(r >= base, r < base + count)

        @pl.when(mine)
        def _():
            keep_copy(r).start()

        @pl.when(jnp.logical_not(mine))
        def _():
            mate_copy(r, mate_base).start()

    for g in range(groups):

        @pl.when(below)
        def _():
            for q in range(g * gw // qw, (g + 1) * gw // qw):
                chain(q)

        if g == groups - 1:

            @pl.when(odd == 1)
            def _():
                rest_up()

        each(blocks, lambda k: finish_group(g, k))
        lax.fori_loop(
            g * PIECES // groups,
            (g + 1) * PIECES // groups,
            lambda r, carry: (share_piece(r), carry)[1],
            0,
        )

    @pl.when(jnp.logical_and(odd == 0, z > 0))
    def _():
        rest_up()

    @pl.when(z == 0)
    def _():
        far_up()

    each(count, lambda k: keep_copy(base + k).wait())

    @pl.when(z == 0)
    def _():
        for v in range(early):
            service(v, 0, count)

    def sib_copy(o, j, c):
        return pltpu.make_async_remote_copy(
            src_ref=part.at[o, j, c, 1 - core],
            dst_ref=sib.at[o, j, c],
            send_sem=sib_send.at[o, j, c],
            recv_sem=sib_recv.at[o, j, c],
            device_id={"head": me + 1 - 2 * core},
            device_id_type=MESH,
        )

    def x_copy(o, j, c, d):
        there = lax.rem(xi + d, xs)
        return pltpu.make_async_remote_copy(
            src_ref=part.at[o, j, c, core, there],
            dst_ref=xbuf.at[d - 1, o, j, c],
            send_sem=x_send.at[d - 1, o, j, c],
            recv_sem=x_recv.at[d - 1, o, j, c],
            device_id={"head": 2 * there + core},
            device_id_type=MESH,
        )

    def z_copy(j, c):
        return pltpu.make_async_remote_copy(
            src_ref=part.at[1, j, c, core, xi],
            dst_ref=zbuf.at[j, c],
            send_sem=z_send.at[j, c],
            recv_sem=z_recv.at[j, c],
            device_id={"ctx": mate},
            device_id_type=MESH,
        )

    def multiply(o, j, c):
        def body(n):
            made = jnp.dot(
                tall[o, :, : n * span], wg[j, c, : n * span, :], preferred_element_type=F32
            ).astype(BF16)
            for h in range(peers):
                part[o, j, c, h % 2, h // 2] = made[h * owned : (h + 1) * owned]

        sized(body)
        sib_copy(o, j, c).start()

    def decode(code):
        o, u = lax.div(code, ctx * chunks), lax.rem(code, ctx * chunks)
        return o, lax.div(u, chunks), lax.rem(u, chunks)

    def chip_sum(code):
        @pl.when(code >= 0)
        def _():
            o, j, c = decode(code)
            sib_copy(o, j, c).wait_recv()
            part[o, j, c, core] = (
                part[o, j, c, core].astype(F32) + sib[o, j, c].astype(F32)
            ).astype(BF16)
            for d in range(1, xs):
                x_copy(o, j, c, d).start()

    def head_sum(code):
        @pl.when(code >= 0)
        def _():
            o, j, c = decode(code)
            sib_copy(o, j, c).wait_send()
            total = part[o, j, c, core, xi].astype(F32)
            for d in range(1, xs):
                x_copy(o, j, c, d).wait()
                total = total + xbuf[d - 1, o, j, c].astype(F32)

            @pl.when(o == 0)
            def _():
                racc[j, c] = total

            @pl.when(o == 1)
            def _():
                part[1, j, c, core, xi] = total.astype(BF16)
                z_copy(j, c).start()

    late = min(MATE_ROUND, units)
    own_kind, line_kind, side_kind = 0, 1, 2
    items = [(0, own_kind, c, 1, 0, 0) for c in range(chunks)]
    for v in range(units + 1):
        if v == late:
            waiting = [(own_kind, c) for c in range(chunks)]
            for w in range(late):
                waiting.append((line_kind, w))
                if share and w:
                    waiting.append((side_kind, w - 1))
            items += [(1, kind, i, 0, 0, int(n == 0)) for n, (kind, i) in enumerate(waiting)]
        turns = [(line_kind, v)] if v < units else []
        if share and v:
            turns.append((side_kind, v - 1))
        for n, (kind, i) in enumerate(turns):
            svc = int(n == 0 and early <= v < units)
            if v >= late:
                items += [(1, kind, i, 1, svc, 0), (0, kind, i, 0, 0, 0)]
            else:
                items.append((0, kind, i, 1, svc, 0))
    size = max(units, chunks)
    table = [
        ((((o * 3 + kind) * size + i) * 2 + new) * 2 + svc) * 2 + hold
        for o, kind, i, new, svc, hold in items
    ]
    closing = [(kind, i) for _, kind, i, *_ in items[-HEAD_LAG:]]
    settled = 0 if any(kind == own_kind for kind, _ in closing) else min(i for _, i in closing)

    def own_done(n):
        c, r = line_chunk(lax.div(n, PIECES)), lax.rem(n, PIECES)
        own_send(True, c, r, lambda node: node >= 0, True)
        own_send(False, c, r, lambda node: node >= 0, True)

    def item(t, carry):
        code = jnp.int32(table[0])
        for n in range(1, len(table)):
            code = jnp.where(t == n, table[n], code)
        hold, code = lax.rem(code, 2), lax.div(code, 2)
        svc, code = lax.rem(code, 2), lax.div(code, 2)
        new, code = lax.rem(code, 2), lax.div(code, 2)
        i, code = lax.rem(code, size), lax.div(code, size)
        kind, o = lax.rem(code, 3), lax.div(code, 3)

        @pl.when(svc == 1)
        def _():
            @pl.when(i == units - 1)
            def _():
                each(line_chunks * PIECES, own_done)
                each(settled, lambda v: service(v, 0, count, True))

            service(i, 0, count)

        @pl.when(hold == 1)
        def _():
            each(count, lambda k: mate_copy(base + k, base).wait_recv())

        _, j, at = unit_of(i)
        own = kind == own_kind
        j = jnp.where(own, z, j)
        c = jnp.where(own, i, line_chunk(at))
        if share:
            c = jnp.where(kind == side_kind, 2 * at + 1 - y, c)

        @pl.when(jnp.logical_and(own, new == 1))
        def _():
            sized(lambda n: local_copy(c, n).wait())

        if share:

            @pl.when(jnp.logical_and(kind == side_kind, new == 1))
            def _():
                each(count, lambda k: arrived(j, c, base + k))

        multiply(o, j, c)
        chip_sum(carry[CHIP_LAG - 1])
        head_sum(carry[HEAD_LAG - 1])
        return ((o * ctx + j) * chunks + c, *carry[:-1])

    none = jnp.int32(-1)
    last = lax.fori_loop(0, len(table), item, (none,) * HEAD_LAG)
    for n in range(CHIP_LAG - 1, -1, -1):
        chip_sum(last[n])

    def collect(u):
        j, c = lax.div(u, chunks), lax.rem(u, chunks)
        z_copy(j, c).wait()
        out_ref[:, rows_of(u, cw)] = (racc[j, c] + zbuf[j, c].astype(F32)).astype(BF16)

    def collect_unit(v):
        _, j, at = unit_of(v)
        collect(j * chunks + line_chunk(at))
        if share:
            collect(j * chunks + 2 * at + 1 - y)

    opened = min(line_chunks, settled)

    def collect_own(when):
        @pl.when(when)
        def _():
            each(chunks, lambda c: collect(z * chunks + c))

    if opened:
        collect_own(odd == 1)
        each(opened, collect_unit)
    for n in range(HEAD_LAG - 1, -1, -1):
        head_sum(last[n])
    each(PIECES - count, lambda k: mate_copy(mate_base + k, mate_base).wait_send())
    if units - 1 < early:
        each(line_chunks * PIECES, own_done)
        each(settled, lambda v: service(v, 0, count, True))
    lax.fori_loop(settled, units, lambda v, carry: (service(v, 0, count, True), carry)[1], 0)

    @pl.when(above)
    def _():
        for q in range(QUARTERS):
            state_copy(q).wait_send()

    collect_own(odd == 0 if opened else odd >= 0)
    lax.fori_loop(opened, units, lambda v, carry: (collect_unit(v), carry)[1], 0)


def shards(
    sizes,
    head_input,
    gate_input,
    input_map,
    output_map,
    step_size,
    decays,
    bypass_scale,
    norm_gain,
    out_weight,
):
    lanes, ctx, peers = sizes
    tokens, width = head_input.shape
    heads = step_size.shape[0]
    blocks = tokens // STRETCH
    depth, cols = out_weight.shape
    cw = min(cols, 256)
    chunks = cols // cw
    owned, xs = tokens // peers, peers // 2
    most = max(SPLIT, PIECES - SPLIT, LAST_SPLIT, PIECES - LAST_SPLIT)
    dma = pltpu.SemaphoreType.DMA
    vmem = pl.BlockSpec(memory_space=pltpu.VMEM)
    anywhere = pl.BlockSpec(memory_space=pl.ANY)
    return pl.pallas_call(
        functools.partial(layer, sizes),
        out_shape=jax.ShapeDtypeStruct((owned, ctx * cols), BF16),
        in_specs=[anywhere] * 4 + [vmem] * 4 + [anywhere],
        out_specs=vmem,
        scratch_shapes=[
            pltpu.VMEM(head_input.shape, BF16),
            pltpu.VMEM(gate_input.shape, BF16),
            pltpu.VMEM(input_map.shape, BF16),
            pltpu.VMEM(output_map.shape, BF16),
            pltpu.VMEM((ctx, chunks, most * depth // PIECES, cw), BF16),
            pltpu.VMEM((2, ctx, chunks, 2, xs, owned, cw), BF16),
            pltpu.VMEM((2, ctx, chunks, xs, owned, cw), BF16),
            pltpu.VMEM((max(xs - 1, 1), 2, ctx, chunks, owned, cw), BF16),
            pltpu.VMEM((ctx, chunks, owned, cw), F32),
            pltpu.VMEM((ctx, chunks, owned, cw), BF16),
            pltpu.VMEM((tokens, width), F32),
            pltpu.VMEM((STATE, width), F32),
            pltpu.VMEM((blocks, STATE, width), BF16),
            pltpu.VMEM((QUARTERS, STATE, width // QUARTERS), BF16),
            pltpu.VMEM((QUARTERS, STATE, width // QUARTERS), BF16),
            pltpu.VMEM((tokens, width), BF16),
            pltpu.VMEM((2, tokens, most * depth // PIECES), BF16),
            pltpu.VMEM((heads, width), BF16),
            pltpu.VMEM((blocks, STRETCH, heads), F32),
            pltpu.VMEM((blocks, heads, STRETCH), F32),
            pltpu.VMEM((blocks, 8, heads), F32),
            pltpu.VMEM((8, heads), F32),
            dma((4,)),
            dma((chunks,)),
            dma((PIECES,)),
            dma((ctx, chunks, PIECES)),
            dma((ctx, chunks, PIECES)),
            dma((ctx, chunks, PIECES)),
            dma((ctx, chunks, PIECES)),
            dma((QUARTERS,)),
            dma((QUARTERS,)),
            dma((PIECES,)),
            dma((PIECES,)),
            dma((2, ctx, chunks)),
            dma((2, ctx, chunks)),
            dma((max(xs - 1, 1), 2, ctx, chunks)),
            dma((max(xs - 1, 1), 2, ctx, chunks)),
            dma((ctx, chunks)),
            dma((ctx, chunks)),
        ],
        compiler_params=pltpu.CompilerParams(
            collective_id=0, has_side_effects=True, vmem_limit_bytes=60 << 20
        ),
    )(
        head_input,
        gate_input,
        input_map,
        output_map,
        step_size,
        decays,
        bypass_scale.reshape(1, heads),
        norm_gain.reshape(1, width),
        out_weight,
    )


def solution(mesh):
    sizes = (mesh.shape["group"], mesh.shape["ctx"], mesh.shape["head"])
    return jax.shard_map(
        functools.partial(shards, sizes),
        mesh=mesh,
        in_specs=(
            P(("group", "ctx"), "head"),
            P(("group", "ctx"), "head"),
            P(("group", "ctx"), "head"),
            P(("group", "ctx"), "head"),
            P("head", ("group", "ctx")),
            P("head", ("group", "ctx")),
            P("head"),
            P("head"),
            P("head", "ctx"),
        ),
        out_specs=P(("group", "ctx", "head"), None),
        check_vma=False,
    )
```

```python
import functools

import jax
import jax.numpy as jnp
from jax import lax
from jax.experimental import pallas as pl
from jax.experimental.pallas import tpu as pltpu
from jax.sharding import PartitionSpec as P

HEADP = 64
STATE = 256
STRETCH = 128
PIECES = 8
SPLIT = 3
LAST_SPLIT = 5
MATE_ROUND = 4
QUARTERS = 8
CHIP_LAG = 2
HEAD_LAG = 8
HEAD_START = 3
MESH = pl.DeviceIdType.MESH
F32 = jnp.float32
BF16 = jnp.bfloat16


def rows_of(k, size):
    return pl.ds(pl.multiple_of(k * size, size), size)


def layer(
    sizes,
    x_any,
    gate_any,
    bm_any,
    cm_any,
    step_ref,
    dec_ref,
    skip_ref,
    gain_ref,
    w_ref,
    out_ref,
    x_ref,
    gate_ref,
    bm_ref,
    cm_ref,
    wg,
    part,
    sib,
    xbuf,
    racc,
    zbuf,
    y_ref,
    st,
    ent,
    inc,
    sbuf,
    normed,
    tall,
    expander,
    ramp_t,
    rows_r,
    lead_ref,
    full_ref,
    load_sem,
    local_sem,
    m_recv,
    w_recv,
    up_send,
    down_send,
    side_send,
    st_send,
    st_recv,
    t_send,
    t_recv,
    sib_send,
    sib_recv,
    x_send,
    x_recv,
    z_send,
    z_recv,
):
    lanes, ctx, peers = sizes
    tokens, width = x_ref.shape
    heads = step_ref.shape[0]
    groups = bm_ref.shape[1] // STATE
    blocks = tokens // STRETCH
    chunks, cw = wg.shape[1], wg.shape[3]
    depth = w_ref.shape[0]
    span = depth // PIECES
    share = lanes == 2 and chunks % 2 == 0
    line_chunks = chunks // 2 if share else chunks
    units = (ctx - 1) * line_chunks
    pairs, xs = ctx // 2, peers // 2
    gw = width // groups
    qw = width // QUARTERS
    owned = tokens // peers
    y, z, me = lax.axis_index("group"), lax.axis_index("ctx"), lax.axis_index("head")
    above, below = z + 1 < ctx, z > 0
    other = {"group": 1 - y} if share else None
    p, odd = lax.div(z, 2), lax.rem(z, 2)
    xi, core = lax.div(me, 2), lax.rem(me, 2)
    mate = z + 1 - 2 * odd

    loads = [
        pltpu.make_async_copy(src, dst, load_sem.at[n])
        for n, (src, dst) in enumerate(
            ((x_any, x_ref), (bm_any, bm_ref), (cm_any, cm_ref), (gate_any, gate_ref))
        )
    ]

    barrier = pltpu.get_barrier_semaphore()

    def greet(target):
        pl.semaphore_signal(barrier, inc=1, device_id=target, device_id_type=MESH)

    met = jnp.int32(0)
    for d in (-2, -1, 1, 2):
        there = jnp.logical_and(z + d >= 0, z + d < ctx)

        @pl.when(there)
        def _():
            greet({"ctx": z + d})

        met = met + jnp.where(there, 1, 0)
    if share:
        greet(other)
    greet({"head": me + 1 - 2 * core})
    for d in range(1, xs):
        greet({"head": 2 * lax.rem(xi + d, xs) + core})
    pl.semaphore_wait(barrier, met + xs + (1 if share else 0))

    for load in loads:
        load.start()

    def split(pair):
        return jnp.where(pair == pairs - 1, LAST_SPLIT, SPLIT)

    def start_of(node):
        return jnp.where(lax.rem(node, 2) == 1, split(lax.div(node, 2)), 0)

    def holder(pair, r):
        return 2 * pair + jnp.where(r >= split(pair), 1, 0)

    cut = split(p)
    base = jnp.where(odd == 1, cut, 0)
    count = jnp.where(odd == 1, PIECES - cut, cut)
    mate_base = jnp.where(odd == 1, 0, cut)

    def sized(body):
        for n in sorted({SPLIT, PIECES - SPLIT, LAST_SPLIT, PIECES - LAST_SPLIT}):

            @pl.when(count == n)
            def _():
                body(n)

    def each(size, body):
        def go(i, carry):
            body(i)
            return carry

        lax.fori_loop(0, size, go, 0)

    def line_chunk(i):
        return 2 * i + y if share else i

    def up_target(r):
        near = jnp.logical_and(odd == 0, r >= cut)
        return jnp.where(near, z + 1, holder(p + 1, r)), jnp.logical_or(near, p + 1 < pairs)

    def down_target(r):
        near = jnp.logical_and(odd == 1, r < cut)
        return jnp.where(near, z - 1, holder(p - 1, r)), jnp.logical_or(near, p > 0)

    def place(j, c, r, node):
        return wg.at[j, c, rows_of(r - start_of(node), span)]

    def send(src, j, c, r, sem, node, target):
        return pltpu.make_async_remote_copy(
            src_ref=src,
            dst_ref=place(j, c, r, node),
            send_sem=sem.at[j, c, r],
            recv_sem=w_recv.at[j, c, r],
            device_id=target,
            device_id_type=MESH,
        )

    def arrived(j, c, r):
        near = {"head": me + 1 - 2 * core}
        send(place(j, c, r, z), j, c, r, up_send, z, near).wait_recv()

    def own_send(up, c, r, want, wait=False):
        node, there = up_target(r) if up else down_target(r)

        @pl.when(jnp.logical_and(there, want(node)))
        def _():
            src = w_ref.at[rows_of(r, span), rows_of(c, cw)]
            copy = send(src, z, c, r, up_send if up else down_send, node, {"ctx": node})
            if wait:
                copy.wait_send()
            else:
                copy.start()

    def own_sends(up, when, far):
        def body(n):
            i, r = lax.div(n, PIECES), lax.rem(n, PIECES)
            r = r if up else PIECES - 1 - r

            def want(node):
                gap = node - z if up else z - node
                return jnp.logical_and(when(i, r), gap == (2 if far else 1))

            own_send(up, line_chunk(i), r, want)

        each(line_chunks * PIECES, body)

    def early_up(i, r):
        few = jnp.logical_and(i == 0, jnp.logical_or(z > 0, r < SPLIT + HEAD_START))
        return jnp.logical_or(few, z == ctx - 2)

    def always(i, r):
        return i >= 0

    own_sends(True, early_up, False)
    own_sends(False, always, False)
    own_sends(False, always, True)

    def rest_up():
        far_up()
        own_sends(True, lambda i, r: jnp.logical_not(early_up(i, r)), False)

    def far_up():
        own_sends(True, always, True)

    def local_copy(c, n):
        return pltpu.make_async_copy(
            w_ref.at[pl.ds(pl.multiple_of(base * span, span), n * span), rows_of(c, cw)],
            wg.at[z, c, pl.ds(0, n * span)],
            local_sem.at[c],
        )

    sized(lambda n: each(chunks, lambda c: local_copy(c, n).start()))

    over, under = ctx - 1 - z, z
    both = jnp.minimum(under, jnp.maximum(over - 1, 0))

    def unit_of(v):
        opening = jnp.logical_and(over > 0, v < line_chunks)
        w = v - jnp.where(over > 0, line_chunks, 0)
        mixed = w < 2 * line_chunks * both
        w = jnp.where(opening, 0, jnp.where(mixed, w, w - 2 * line_chunks * both))
        within = lax.rem(w, 2 * line_chunks)
        s = jnp.where(mixed, lax.div(w, 2 * line_chunks), both + lax.div(w, line_chunks)) + 1
        i = jnp.where(mixed, lax.div(within, 2), lax.rem(w, line_chunks))
        falling = jnp.where(mixed, lax.rem(within, 2) == 1, over - 1 > both)
        s = jnp.where(opening, 0, s)
        i = jnp.where(opening, v, i)
        falling = jnp.logical_or(opening, falling)
        return falling, jnp.where(falling, z + 1 + s, z - s), i

    def service(v, lo, hi, wait=False):
        falling, j, i = unit_of(v)
        c = line_chunk(i)

        def body(k):
            r = base + jnp.where(falling, count - 1 - k, k)
            if not wait:
                arrived(j, c, r)
            for up in (True, False):
                node, there = up_target(r) if up else down_target(r)
                there = jnp.logical_and(there, jnp.logical_xor(falling, up))

                @pl.when(there)
                def _():
                    sem = up_send if up else down_send
                    copy = send(place(j, c, r, z), j, c, r, sem, node, {"ctx": node})
                    if wait:
                        copy.wait_send()
                    else:
                        copy.start()

            if share:
                copy = send(place(j, c, r, z), j, c, r, side_send, z, other)
                if wait:
                    copy.wait_send()
                else:
                    copy.start()

        lax.fori_loop(lo, hi, lambda k, carry: (body(k), carry)[1], 0)

    spots = lax.broadcasted_iota(jnp.int32, (heads, width), 1)
    owner = lax.broadcasted_iota(jnp.int32, (heads, width), 0)
    inside = jnp.logical_and(spots >= owner * HEADP, spots < owner * HEADP + HEADP)
    expander[...] = jnp.where(inside, 1.0, 0.0).astype(BF16)

    def spread(v, lo, size):
        high = v.astype(BF16)
        low = (v - high.astype(F32)).astype(BF16)
        e = expander[:, lo : lo + size]
        return jnp.dot(high, e, preferred_element_type=F32) + jnp.dot(
            low, e, preferred_element_type=F32
        )

    row_i = lax.broadcasted_iota(jnp.int32, (STRETCH, STRETCH), 0)
    col_i = lax.broadcasted_iota(jnp.int32, (STRETCH, STRETCH), 1)
    lower = row_i >= col_i
    nt = (((1,), (1,)), ((), ()))
    tn = (((0,), (0,)), ((), ()))

    st[...] = jnp.zeros_like(st)

    def states(k, lead):
        rows = rows_of(k, STRETCH)
        low_tri = jnp.where(lower, 1.0, 0.0).astype(F32)
        eye = jnp.where(row_i == col_i, 1.0, 0.0).astype(F32)
        logd = jnp.log(dec_ref[:, rows])
        logs = jnp.log(step_ref[:, rows])
        exact = functools.partial(
            lax.dot_general,
            dimension_numbers=nt,
            precision=lax.Precision.HIGHEST,
            preferred_element_type=F32,
        )
        ramp = exact(logd, low_tri)
        rt = exact(low_tri, logd)
        st_t = exact(eye, logs)
        rows_r[k] = ramp - logs
        ramp_t[k] = rt
        lead_ref[k] = lead
        end = rt[STRETCH - 1 : STRETCH, :]
        tails = jnp.exp(end - (rt - st_t))
        total = jnp.broadcast_to(jnp.exp(end), (8, heads))
        for g in range(groups):
            cols = slice(g * gw, (g + 1) * gw)
            weighted = (x_ref[rows, cols].astype(F32) * spread(tails, g * gw, gw)).astype(BF16)
            made = lax.dot_general(
                bm_ref[rows, g * STATE : (g + 1) * STATE],
                weighted,
                tn,
                preferred_element_type=F32,
            )
            old = st[:, cols]
            ent[k, :, cols] = old.astype(BF16)
            st[:, cols] = spread(total, g * gw, gw)[0:1] * old + made
        return lead + jnp.broadcast_to(end, (8, heads))

    loads[0].wait()
    loads[1].wait()
    lead = lax.fori_loop(0, blocks, states, jnp.zeros((8, heads), F32))
    full_ref[...] = jnp.exp(lead)

    def state_copy(q):
        return pltpu.make_async_remote_copy(
            src_ref=sbuf.at[q],
            dst_ref=inc.at[q],
            send_sem=st_send.at[q],
            recv_sem=st_recv.at[q],
            device_id={"ctx": z + 1},
            device_id_type=MESH,
        )

    @pl.when(z == 0)
    def _():
        for q in range(QUARTERS):
            inc[q] = jnp.zeros_like(inc[q])
            sbuf[q] = st[:, q * qw : (q + 1) * qw].astype(BF16)

            @pl.when(above)
            def _():
                state_copy(q).start()

        own_sends(True, lambda i, r: jnp.logical_not(early_up(i, r)), False)

    early = min(2, units)
    stage = QUARTERS // 2

    def chain(q):
        if q // stage < early:
            at = q % stage
            service(q // stage, at, count if at == stage - 1 else jnp.minimum(at + 1, count))
        pltpu.make_async_remote_copy(
            src_ref=sbuf.at[q],
            dst_ref=inc.at[q],
            send_sem=st_send.at[q],
            recv_sem=st_recv.at[q],
            device_id={"ctx": z - 1},
            device_id_type=MESH,
        ).wait_recv()

        @pl.when(above)
        def _():
            fall = spread(full_ref[...], q * qw, qw)[0:1]
            held = st[:, q * qw : (q + 1) * qw]
            sbuf[q] = (fall * inc[q].astype(F32) + held).astype(BF16)
            state_copy(q).start()

    half = lax.broadcasted_iota(jnp.int32, (STRETCH, 2 * HEADP), 1) < HEADP
    keep_lo = jnp.where(half, 1.0, 0.0).astype(BF16)
    keep_hi = jnp.where(half, 0.0, 1.0).astype(BF16)
    per_group = heads // groups

    def own_block(k, carry):
        rows = rows_of(k, STRETCH)
        rt = ramp_t[k]
        rr = rows_r[k]
        entry = jnp.exp(rt)
        for g in range(groups):
            c_map = cm_ref[rows, g * STATE : (g + 1) * STATE]
            b_map = bm_ref[rows, g * STATE : (g + 1) * STATE]
            scores = lax.dot_general(c_map, b_map, nt, preferred_element_type=F32)
            cols = slice(g * gw, (g + 1) * gw)
            skip = spread(jnp.broadcast_to(skip_ref[...], (8, heads)), g * gw, gw)[0:1]
            y_ref[rows, cols] = (
                jnp.dot(c_map, ent[k, :, cols], preferred_element_type=F32)
                * spread(entry, g * gw, gw)
                + skip * x_ref[rows, cols].astype(F32)
            )
            for pair in range(per_group // 2):
                mixes = []
                for h in (g * per_group + 2 * pair, g * per_group + 2 * pair + 1):
                    fade = jnp.where(lower, rt[:, h : h + 1] - rr[h : h + 1, :], -1e30)
                    mixes.append((scores * jnp.exp(fade)).astype(BF16))
                at = slice(g * gw + pair * 2 * HEADP, g * gw + (pair + 1) * 2 * HEADP)
                both = x_ref[rows, at]
                y_ref[rows, at] += jnp.dot(
                    jnp.concatenate(mixes, axis=1),
                    jnp.concatenate([both * keep_lo, both * keep_hi], axis=0),
                    preferred_element_type=F32,
                )

        return carry

    loads[2].wait()
    lax.fori_loop(0, blocks, own_block, 0)
    loads[3].wait()

    def finish_group(g, k):
        rows = rows_of(k, STRETCH)
        reach = jnp.exp(ramp_t[k] + lead_ref[k, 0:1])
        squares = jnp.zeros((STRETCH, 1), F32)
        for q in range(g * gw // qw, (g + 1) * gw // qw):
            cols = slice(q * qw, (q + 1) * qw)
            carried = jnp.dot(
                cm_ref[rows, g * STATE : (g + 1) * STATE], inc[q], preferred_element_type=F32
            )
            gate = gate_ref[rows, cols].astype(F32)
            gated = (y_ref[rows, cols] + carried * spread(reach, q * qw, qw)) * (
                gate / (1.0 + jnp.exp(-gate))
            )
            y_ref[rows, cols] = gated
            squares = squares + jnp.sum(gated * gated, axis=1, keepdims=True)
        cols = slice(g * gw, (g + 1) * gw)
        factor = lax.rsqrt(squares / gw + 1e-05)
        normed[rows, cols] = (y_ref[rows, cols] * factor * gain_ref[:, cols].astype(F32)).astype(
            BF16
        )

    def keep_copy(r):
        return pltpu.make_async_copy(
            normed.at[:, rows_of(r, span)], tall.at[0, :, rows_of(r - base, span)], t_recv.at[r]
        )

    def mate_copy(r, start):
        return pltpu.make_async_remote_copy(
            src_ref=normed.at[:, rows_of(r, span)],
            dst_ref=tall.at[1, :, rows_of(r - start, span)],
            send_sem=t_send.at[r],
            recv_sem=m_recv.at[r],
            device_id={"ctx": mate},
            device_id_type=MESH,
        )

    def share_piece(r):
        mine = jnp.logical_and(r >= base, r < base + count)

        @pl.when(mine)
        def _():
            keep_copy(r).start()

        @pl.when(jnp.logical_not(mine))
        def _():
            mate_copy(r, mate_base).start()

    for g in range(groups):

        @pl.when(below)
        def _():
            for q in range(g * gw // qw, (g + 1) * gw // qw):
                chain(q)

        if g == groups - 1:

            @pl.when(odd == 1)
            def _():
                rest_up()

        each(blocks, lambda k: finish_group(g, k))
        lax.fori_loop(
            g * PIECES // groups,
            (g + 1) * PIECES // groups,
            lambda r, carry: (share_piece(r), carry)[1],
            0,
        )

    @pl.when(jnp.logical_and(odd == 0, z > 0))
    def _():
        rest_up()

    @pl.when(z == 0)
    def _():
        far_up()

    each(count, lambda k: keep_copy(base + k).wait())

    @pl.when(z == 0)
    def _():
        for v in range(early):
            service(v, 0, count)

    def sib_copy(o, j, c):
        return pltpu.make_async_remote_copy(
            src_ref=part.at[o, j, c, 1 - core],
            dst_ref=sib.at[o, j, c],
            send_sem=sib_send.at[o, j, c],
            recv_sem=sib_recv.at[o, j, c],
            device_id={"head": me + 1 - 2 * core},
            device_id_type=MESH,
        )

    def x_copy(o, j, c, d):
        there = lax.rem(xi + d, xs)
        return pltpu.make_async_remote_copy(
            src_ref=part.at[o, j, c, core, there],
            dst_ref=xbuf.at[d - 1, o, j, c],
            send_sem=x_send.at[d - 1, o, j, c],
            recv_sem=x_recv.at[d - 1, o, j, c],
            device_id={"head": 2 * there + core},
            device_id_type=MESH,
        )

    def z_copy(j, c):
        return pltpu.make_async_remote_copy(
            src_ref=part.at[1, j, c, core, xi],
            dst_ref=zbuf.at[j, c],
            send_sem=z_send.at[j, c],
            recv_sem=z_recv.at[j, c],
            device_id={"ctx": mate},
            device_id_type=MESH,
        )

    def multiply(o, j, c):
        def body(n):
            made = jnp.dot(
                tall[o, :, : n * span], wg[j, c, : n * span, :], preferred_element_type=F32
            ).astype(BF16)
            for h in range(peers):
                part[o, j, c, h % 2, h // 2] = made[h * owned : (h + 1) * owned]

        sized(body)
        sib_copy(o, j, c).start()

    def decode(code):
        o, u = lax.div(code, ctx * chunks), lax.rem(code, ctx * chunks)
        return o, lax.div(u, chunks), lax.rem(u, chunks)

    def chip_sum(code):
        @pl.when(code >= 0)
        def _():
            o, j, c = decode(code)
            sib_copy(o, j, c).wait_recv()
            part[o, j, c, core] = (
                part[o, j, c, core].astype(F32) + sib[o, j, c].astype(F32)
            ).astype(BF16)
            for d in range(1, xs):
                x_copy(o, j, c, d).start()

    def head_sum(code):
        @pl.when(code >= 0)
        def _():
            o, j, c = decode(code)
            sib_copy(o, j, c).wait_send()
            total = part[o, j, c, core, xi].astype(F32)
            for d in range(1, xs):
                x_copy(o, j, c, d).wait()
                total = total + xbuf[d - 1, o, j, c].astype(F32)

            @pl.when(o == 0)
            def _():
                racc[j, c] = total

            @pl.when(o == 1)
            def _():
                part[1, j, c, core, xi] = total.astype(BF16)
                z_copy(j, c).start()

    late = min(MATE_ROUND, units)
    own_kind, line_kind, side_kind = 0, 1, 2
    items = [(0, own_kind, c, 1, 0, 0) for c in range(chunks)]
    for v in range(units + 1):
        if v == late:
            waiting = [(own_kind, c) for c in range(chunks)]
            for w in range(late):
                waiting.append((line_kind, w))
                if share and w:
                    waiting.append((side_kind, w - 1))
            items += [(1, kind, i, 0, 0, int(n == 0)) for n, (kind, i) in enumerate(waiting)]
        turns = [(line_kind, v)] if v < units else []
        if share and v:
            turns.append((side_kind, v - 1))
        for n, (kind, i) in enumerate(turns):
            svc = int(n == 0 and early <= v < units)
            if v >= late:
                items += [(1, kind, i, 1, svc, 0), (0, kind, i, 0, 0, 0)]
            else:
                items.append((0, kind, i, 1, svc, 0))
    size = max(units, chunks)
    table = [
        ((((o * 3 + kind) * size + i) * 2 + new) * 2 + svc) * 2 + hold
        for o, kind, i, new, svc, hold in items
    ]
    closing = [(kind, i) for _, kind, i, *_ in items[-HEAD_LAG:]]
    settled = 0 if any(kind == own_kind for kind, _ in closing) else min(i for _, i in closing)

    def own_done(n):
        c, r = line_chunk(lax.div(n, PIECES)), lax.rem(n, PIECES)
        own_send(True, c, r, lambda node: node >= 0, True)
        own_send(False, c, r, lambda node: node >= 0, True)

    def item(t, carry):
        code = jnp.int32(table[0])
        for n in range(1, len(table)):
            code = jnp.where(t == n, table[n], code)
        hold, code = lax.rem(code, 2), lax.div(code, 2)
        svc, code = lax.rem(code, 2), lax.div(code, 2)
        new, code = lax.rem(code, 2), lax.div(code, 2)
        i, code = lax.rem(code, size), lax.div(code, size)
        kind, o = lax.rem(code, 3), lax.div(code, 3)

        @pl.when(svc == 1)
        def _():
            @pl.when(i == units - 1)
            def _():
                each(line_chunks * PIECES, own_done)
                each(settled, lambda v: service(v, 0, count, True))

            service(i, 0, count)

        @pl.when(hold == 1)
        def _():
            each(count, lambda k: mate_copy(base + k, base).wait_recv())

        _, j, at = unit_of(i)
        own = kind == own_kind
        j = jnp.where(own, z, j)
        c = jnp.where(own, i, line_chunk(at))
        if share:
            c = jnp.where(kind == side_kind, 2 * at + 1 - y, c)

        @pl.when(jnp.logical_and(own, new == 1))
        def _():
            sized(lambda n: local_copy(c, n).wait())

        if share:

            @pl.when(jnp.logical_and(kind == side_kind, new == 1))
            def _():
                each(count, lambda k: arrived(j, c, base + k))

        multiply(o, j, c)
        chip_sum(carry[CHIP_LAG - 1])
        head_sum(carry[HEAD_LAG - 1])
        return ((o * ctx + j) * chunks + c, *carry[:-1])

    none = jnp.int32(-1)
    last = lax.fori_loop(0, len(table), item, (none,) * HEAD_LAG)
    for n in range(CHIP_LAG - 1, -1, -1):
        chip_sum(last[n])

    def collect(u):
        j, c = lax.div(u, chunks), lax.rem(u, chunks)
        z_copy(j, c).wait()
        out_ref[:, rows_of(u, cw)] = (racc[j, c] + zbuf[j, c].astype(F32)).astype(BF16)

    def collect_unit(v):
        _, j, at = unit_of(v)
        collect(j * chunks + line_chunk(at))
        if share:
            collect(j * chunks + 2 * at + 1 - y)

    opened = min(line_chunks, settled)

    def collect_own(when):
        @pl.when(when)
        def _():
            each(chunks, lambda c: collect(z * chunks + c))

    if opened:
        collect_own(odd == 1)
        each(opened, collect_unit)
    for n in range(HEAD_LAG - 1, -1, -1):
        head_sum(last[n])
    each(PIECES - count, lambda k: mate_copy(mate_base + k, mate_base).wait_send())
    if units - 1 < early:
        each(line_chunks * PIECES, own_done)
        each(settled, lambda v: service(v, 0, count, True))
    lax.fori_loop(settled, units, lambda v, carry: (service(v, 0, count, True), carry)[1], 0)

    @pl.when(above)
    def _():
        for q in range(QUARTERS):
            state_copy(q).wait_send()

    collect_own(odd == 0 if opened else odd >= 0)
    lax.fori_loop(opened, units, lambda v, carry: (collect_unit(v), carry)[1], 0)


def shards(
    sizes,
    head_input,
    gate_input,
    input_map,
    output_map,
    step_size,
    decays,
    bypass_scale,
    norm_gain,
    out_weight,
):
    lanes, ctx, peers = sizes
    tokens, width = head_input.shape
    heads = step_size.shape[0]
    blocks = tokens // STRETCH
    depth, cols = out_weight.shape
    cw = min(cols, 256)
    chunks = cols // cw
    owned, xs = tokens // peers, peers // 2
    most = max(SPLIT, PIECES - SPLIT, LAST_SPLIT, PIECES - LAST_SPLIT)
    dma = pltpu.SemaphoreType.DMA
    vmem = pl.BlockSpec(memory_space=pltpu.VMEM)
    anywhere = pl.BlockSpec(memory_space=pl.ANY)
    return pl.pallas_call(
        functools.partial(layer, sizes),
        out_shape=jax.ShapeDtypeStruct((owned, ctx * cols), BF16),
        in_specs=[anywhere] * 4 + [vmem] * 4 + [anywhere],
        out_specs=vmem,
        scratch_shapes=[
            pltpu.VMEM(head_input.shape, BF16),
            pltpu.VMEM(gate_input.shape, BF16),
            pltpu.VMEM(input_map.shape, BF16),
            pltpu.VMEM(output_map.shape, BF16),
            pltpu.VMEM((ctx, chunks, most * depth // PIECES, cw), BF16),
            pltpu.VMEM((2, ctx, chunks, 2, xs, owned, cw), BF16),
            pltpu.VMEM((2, ctx, chunks, xs, owned, cw), BF16),
            pltpu.VMEM((max(xs - 1, 1), 2, ctx, chunks, owned, cw), BF16),
            pltpu.VMEM((ctx, chunks, owned, cw), F32),
            pltpu.VMEM((ctx, chunks, owned, cw), BF16),
            pltpu.VMEM((tokens, width), F32),
            pltpu.VMEM((STATE, width), F32),
            pltpu.VMEM((blocks, STATE, width), BF16),
            pltpu.VMEM((QUARTERS, STATE, width // QUARTERS), BF16),
            pltpu.VMEM((QUARTERS, STATE, width // QUARTERS), BF16),
            pltpu.VMEM((tokens, width), BF16),
            pltpu.VMEM((2, tokens, most * depth // PIECES), BF16),
            pltpu.VMEM((heads, width), BF16),
            pltpu.VMEM((blocks, STRETCH, heads), F32),
            pltpu.VMEM((blocks, heads, STRETCH), F32),
            pltpu.VMEM((blocks, 8, heads), F32),
            pltpu.VMEM((8, heads), F32),
            dma((4,)),
            dma((chunks,)),
            dma((PIECES,)),
            dma((ctx, chunks, PIECES)),
            dma((ctx, chunks, PIECES)),
            dma((ctx, chunks, PIECES)),
            dma((ctx, chunks, PIECES)),
            dma((QUARTERS,)),
            dma((QUARTERS,)),
            dma((PIECES,)),
            dma((PIECES,)),
            dma((2, ctx, chunks)),
            dma((2, ctx, chunks)),
            dma((max(xs - 1, 1), 2, ctx, chunks)),
            dma((max(xs - 1, 1), 2, ctx, chunks)),
            dma((ctx, chunks)),
            dma((ctx, chunks)),
        ],
        compiler_params=pltpu.CompilerParams(
            collective_id=0, has_side_effects=True, vmem_limit_bytes=60 << 20
        ),
    )(
        head_input,
        gate_input,
        input_map,
        output_map,
        step_size,
        decays,
        bypass_scale.reshape(1, heads),
        norm_gain.reshape(1, width),
        out_weight,
    )


def solution(mesh):
    sizes = (mesh.shape["group"], mesh.shape["ctx"], mesh.shape["head"])
    return jax.shard_map(
        functools.partial(shards, sizes),
        mesh=mesh,
        in_specs=(
            P(("group", "ctx"), "head"),
            P(("group", "ctx"), "head"),
            P(("group", "ctx"), "head"),
            P(("group", "ctx"), "head"),
            P("head", ("group", "ctx")),
            P("head", ("group", "ctx")),
            P("head"),
            P("head"),
            P("head", "ctx"),
        ),
        out_specs=P(("group", "ctx", "head"), None),
        check_vma=False,
    )
```

```python
import functools

import jax
import jax.numpy as jnp
from jax import lax
from jax.experimental import pallas as pl
from jax.experimental.pallas import tpu as pltpu
from jax.sharding import PartitionSpec as P

HEADP = 64
STATE = 256
STRETCH = 128
PIECES = 8
SPLIT = 3
LAST_SPLIT = 5
MATE_ROUND = 4
QUARTERS = 4
CHIP_LAG = 2
HEAD_LAG = 8
HEAD_START = 3
MESH = pl.DeviceIdType.MESH
F32 = jnp.float32
BF16 = jnp.bfloat16


def rows_of(k, size):
    return pl.ds(pl.multiple_of(k * size, size), size)


def layer(
    sizes,
    x_any,
    gate_any,
    bm_any,
    cm_any,
    step_ref,
    dec_ref,
    skip_ref,
    gain_ref,
    w_ref,
    out_ref,
    x_ref,
    gate_ref,
    bm_ref,
    cm_ref,
    wg,
    part,
    sib,
    xbuf,
    racc,
    zbuf,
    y_ref,
    st,
    ent,
    inc,
    sbuf,
    normed,
    tall,
    expander,
    ramp_t,
    rows_r,
    lead_ref,
    full_ref,
    load_sem,
    local_sem,
    m_recv,
    w_recv,
    up_send,
    down_send,
    side_send,
    st_send,
    st_recv,
    t_send,
    t_recv,
    sib_send,
    sib_recv,
    x_send,
    x_recv,
    z_send,
    z_recv,
):
    lanes, ctx, peers = sizes
    tokens, width = x_ref.shape
    heads = step_ref.shape[0]
    groups = bm_ref.shape[1] // STATE
    blocks = tokens // STRETCH
    chunks, cw = wg.shape[1], wg.shape[3]
    depth = w_ref.shape[0]
    span = depth // PIECES
    share = lanes == 2 and chunks % 2 == 0
    line_chunks = chunks // 2 if share else chunks
    units = (ctx - 1) * line_chunks
    pairs, xs = ctx // 2, peers // 2
    gw = width // groups
    qw = width // QUARTERS
    owned = tokens // peers
    y, z, me = lax.axis_index("group"), lax.axis_index("ctx"), lax.axis_index("head")
    above, below = z + 1 < ctx, z > 0
    other = {"group": 1 - y} if share else None
    p, odd = lax.div(z, 2), lax.rem(z, 2)
    xi, core = lax.div(me, 2), lax.rem(me, 2)
    mate = z + 1 - 2 * odd

    loads = [
        pltpu.make_async_copy(src, dst, load_sem.at[n])
        for n, (src, dst) in enumerate(
            ((x_any, x_ref), (bm_any, bm_ref), (cm_any, cm_ref), (gate_any, gate_ref))
        )
    ]

    barrier = pltpu.get_barrier_semaphore()

    def greet(target):
        pl.semaphore_signal(barrier, inc=1, device_id=target, device_id_type=MESH)

    met = jnp.int32(0)
    for d in (-2, -1, 1, 2):
        there = jnp.logical_and(z + d >= 0, z + d < ctx)

        @pl.when(there)
        def _():
            greet({"ctx": z + d})

        met = met + jnp.where(there, 1, 0)
    if share:
        greet(other)
    greet({"head": me + 1 - 2 * core})
    for d in range(1, xs):
        greet({"head": 2 * lax.rem(xi + d, xs) + core})
    pl.semaphore_wait(barrier, met + xs + (1 if share else 0))

    for load in loads:
        load.start()

    def split(pair):
        return jnp.where(pair == pairs - 1, LAST_SPLIT, SPLIT)

    def start_of(node):
        return jnp.where(lax.rem(node, 2) == 1, split(lax.div(node, 2)), 0)

    def holder(pair, r):
        return 2 * pair + jnp.where(r >= split(pair), 1, 0)

    cut = split(p)
    base = jnp.where(odd == 1, cut, 0)
    count = jnp.where(odd == 1, PIECES - cut, cut)
    mate_base = jnp.where(odd == 1, 0, cut)

    def sized(body):
        for n in sorted({SPLIT, PIECES - SPLIT, LAST_SPLIT, PIECES - LAST_SPLIT}):

            @pl.when(count == n)
            def _():
                body(n)

    def each(size, body):
        def go(i, carry):
            body(i)
            return carry

        lax.fori_loop(0, size, go, 0)

    def line_chunk(i):
        return 2 * i + y if share else i

    def up_target(r):
        near = jnp.logical_and(odd == 0, r >= cut)
        return jnp.where(near, z + 1, holder(p + 1, r)), jnp.logical_or(near, p + 1 < pairs)

    def down_target(r):
        near = jnp.logical_and(odd == 1, r < cut)
        return jnp.where(near, z - 1, holder(p - 1, r)), jnp.logical_or(near, p > 0)

    def place(j, c, r, node):
        return wg.at[j, c, rows_of(r - start_of(node), span)]

    def send(src, j, c, r, sem, node, target):
        return pltpu.make_async_remote_copy(
            src_ref=src,
            dst_ref=place(j, c, r, node),
            send_sem=sem.at[j, c, r],
            recv_sem=w_recv.at[j, c, r],
            device_id=target,
            device_id_type=MESH,
        )

    def arrived(j, c, r):
        near = {"head": me + 1 - 2 * core}
        send(place(j, c, r, z), j, c, r, up_send, z, near).wait_recv()

    def own_send(up, c, r, want, wait=False):
        node, there = up_target(r) if up else down_target(r)

        @pl.when(jnp.logical_and(there, want(node)))
        def _():
            src = w_ref.at[rows_of(r, span), rows_of(c, cw)]
            copy = send(src, z, c, r, up_send if up else down_send, node, {"ctx": node})
            if wait:
                copy.wait_send()
            else:
                copy.start()

    def own_sends(up, when, far):
        def body(n):
            i, r = lax.div(n, PIECES), lax.rem(n, PIECES)
            r = r if up else PIECES - 1 - r

            def want(node):
                gap = node - z if up else z - node
                return jnp.logical_and(when(i, r), gap == (2 if far else 1))

            own_send(up, line_chunk(i), r, want)

        each(line_chunks * PIECES, body)

    def early_up(i, r):
        few = jnp.logical_and(i == 0, jnp.logical_or(z > 0, r < SPLIT + HEAD_START))
        return jnp.logical_or(few, z == ctx - 2)

    def always(i, r):
        return i >= 0

    own_sends(True, early_up, False)
    own_sends(False, always, False)
    own_sends(False, always, True)

    def rest_up():
        far_up()
        own_sends(True, lambda i, r: jnp.logical_not(early_up(i, r)), False)

    def far_up():
        own_sends(True, always, True)

    def local_copy(c, n):
        return pltpu.make_async_copy(
            w_ref.at[pl.ds(pl.multiple_of(base * span, span), n * span), rows_of(c, cw)],
            wg.at[z, c, pl.ds(0, n * span)],
            local_sem.at[c],
        )

    sized(lambda n: each(chunks, lambda c: local_copy(c, n).start()))

    over, under = ctx - 1 - z, z
    both = jnp.minimum(under, jnp.maximum(over - 1, 0))

    def unit_of(v):
        opening = jnp.logical_and(over > 0, v < line_chunks)
        w = v - jnp.where(over > 0, line_chunks, 0)
        mixed = w < 2 * line_chunks * both
        w = jnp.where(opening, 0, jnp.where(mixed, w, w - 2 * line_chunks * both))
        within = lax.rem(w, 2 * line_chunks)
        s = jnp.where(mixed, lax.div(w, 2 * line_chunks), both + lax.div(w, line_chunks)) + 1
        i = jnp.where(mixed, lax.div(within, 2), lax.rem(w, line_chunks))
        falling = jnp.where(mixed, lax.rem(within, 2) == 1, over - 1 > both)
        s = jnp.where(opening, 0, s)
        i = jnp.where(opening, v, i)
        falling = jnp.logical_or(opening, falling)
        return falling, jnp.where(falling, z + 1 + s, z - s), i

    def service(v, lo, hi, wait=False):
        falling, j, i = unit_of(v)
        c = line_chunk(i)

        def body(k):
            r = base + jnp.where(falling, count - 1 - k, k)
            if not wait:
                arrived(j, c, r)
            for up in (True, False):
                node, there = up_target(r) if up else down_target(r)
                there = jnp.logical_and(there, jnp.logical_xor(falling, up))

                @pl.when(there)
                def _():
                    sem = up_send if up else down_send
                    copy = send(place(j, c, r, z), j, c, r, sem, node, {"ctx": node})
                    if wait:
                        copy.wait_send()
                    else:
                        copy.start()

            if share:
                copy = send(place(j, c, r, z), j, c, r, side_send, z, other)
                if wait:
                    copy.wait_send()
                else:
                    copy.start()

        lax.fori_loop(lo, hi, lambda k, carry: (body(k), carry)[1], 0)

    spots = lax.broadcasted_iota(jnp.int32, (heads, width), 1)
    owner = lax.broadcasted_iota(jnp.int32, (heads, width), 0)
    inside = jnp.logical_and(spots >= owner * HEADP, spots < owner * HEADP + HEADP)
    expander[...] = jnp.where(inside, 1.0, 0.0).astype(BF16)

    def spread(v, lo, size):
        high = v.astype(BF16)
        low = (v - high.astype(F32)).astype(BF16)
        e = expander[:, lo : lo + size]
        return jnp.dot(high, e, preferred_element_type=F32) + jnp.dot(
            low, e, preferred_element_type=F32
        )

    row_i = lax.broadcasted_iota(jnp.int32, (STRETCH, STRETCH), 0)
    col_i = lax.broadcasted_iota(jnp.int32, (STRETCH, STRETCH), 1)
    lower = row_i >= col_i
    nt = (((1,), (1,)), ((), ()))
    tn = (((0,), (0,)), ((), ()))

    st[...] = jnp.zeros_like(st)

    def states(k, lead):
        rows = rows_of(k, STRETCH)
        low_tri = jnp.where(lower, 1.0, 0.0).astype(F32)
        eye = jnp.where(row_i == col_i, 1.0, 0.0).astype(F32)
        logd = jnp.log(dec_ref[:, rows])
        logs = jnp.log(step_ref[:, rows])
        exact = functools.partial(
            lax.dot_general,
            dimension_numbers=nt,
            precision=lax.Precision.HIGHEST,
            preferred_element_type=F32,
        )
        ramp = exact(logd, low_tri)
        rt = exact(low_tri, logd)
        st_t = exact(eye, logs)
        rows_r[k] = ramp - logs
        ramp_t[k] = rt
        lead_ref[k] = lead
        end = rt[STRETCH - 1 : STRETCH, :]
        tails = jnp.exp(end - (rt - st_t))
        total = jnp.broadcast_to(jnp.exp(end), (8, heads))
        for g in range(groups):
            cols = slice(g * gw, (g + 1) * gw)
            weighted = (x_ref[rows, cols].astype(F32) * spread(tails, g * gw, gw)).astype(BF16)
            made = lax.dot_general(
                bm_ref[rows, g * STATE : (g + 1) * STATE],
                weighted,
                tn,
                preferred_element_type=F32,
            )
            old = st[:, cols]
            ent[k, :, cols] = old.astype(BF16)
            st[:, cols] = spread(total, g * gw, gw)[0:1] * old + made
        return lead + jnp.broadcast_to(end, (8, heads))

    loads[0].wait()
    loads[1].wait()
    lead = lax.fori_loop(0, blocks, states, jnp.zeros((8, heads), F32))
    full_ref[...] = jnp.exp(lead)

    def state_copy(q):
        return pltpu.make_async_remote_copy(
            src_ref=sbuf.at[q],
            dst_ref=inc.at[q],
            send_sem=st_send.at[q],
            recv_sem=st_recv.at[q],
            device_id={"ctx": z + 1},
            device_id_type=MESH,
        )

    @pl.when(z == 0)
    def _():
        for q in range(QUARTERS):
            inc[q] = jnp.zeros_like(inc[q])
            sbuf[q] = st[:, q * qw : (q + 1) * qw].astype(BF16)

            @pl.when(above)
            def _():
                state_copy(q).start()

        own_sends(True, lambda i, r: jnp.logical_not(early_up(i, r)), False)

    early = min(2, units)
    stage = QUARTERS // 2

    def chain(q):
        if q // stage < early:
            at = q % stage
            service(q // stage, at, count if at == stage - 1 else jnp.minimum(at + 1, count))
        pltpu.make_async_remote_copy(
            src_ref=sbuf.at[q],
            dst_ref=inc.at[q],
            send_sem=st_send.at[q],
            recv_sem=st_recv.at[q],
            device_id={"ctx": z - 1},
            device_id_type=MESH,
        ).wait_recv()

        @pl.when(above)
        def _():
            fall = spread(full_ref[...], q * qw, qw)[0:1]
            held = st[:, q * qw : (q + 1) * qw]
            sbuf[q] = (fall * inc[q].astype(F32) + held).astype(BF16)
            state_copy(q).start()

    half = lax.broadcasted_iota(jnp.int32, (STRETCH, 2 * HEADP), 1) < HEADP
    keep_lo = jnp.where(half, 1.0, 0.0).astype(BF16)
    keep_hi = jnp.where(half, 0.0, 1.0).astype(BF16)
    per_group = heads // groups

    def own_block(k, carry):
        rows = rows_of(k, STRETCH)
        rt = ramp_t[k]
        rr = rows_r[k]
        entry = jnp.exp(rt)
        for g in range(groups):
            c_map = cm_ref[rows, g * STATE : (g + 1) * STATE]
            b_map = bm_ref[rows, g * STATE : (g + 1) * STATE]
            scores = lax.dot_general(c_map, b_map, nt, preferred_element_type=F32)
            cols = slice(g * gw, (g + 1) * gw)
            skip = spread(jnp.broadcast_to(skip_ref[...], (8, heads)), g * gw, gw)[0:1]
            y_ref[rows, cols] = (
                jnp.dot(c_map, ent[k, :, cols], preferred_element_type=F32)
                * spread(entry, g * gw, gw)
                + skip * x_ref[rows, cols].astype(F32)
            )
            for pair in range(per_group // 2):
                mixes = []
                for h in (g * per_group + 2 * pair, g * per_group + 2 * pair + 1):
                    fade = jnp.where(lower, rt[:, h : h + 1] - rr[h : h + 1, :], -1e30)
                    mixes.append((scores * jnp.exp(fade)).astype(BF16))
                at = slice(g * gw + pair * 2 * HEADP, g * gw + (pair + 1) * 2 * HEADP)
                both = x_ref[rows, at]
                y_ref[rows, at] += jnp.dot(
                    jnp.concatenate(mixes, axis=1),
                    jnp.concatenate([both * keep_lo, both * keep_hi], axis=0),
                    preferred_element_type=F32,
                )

        return carry

    loads[2].wait()
    lax.fori_loop(0, blocks, own_block, 0)
    loads[3].wait()

    def finish_group(g, k):
        rows = rows_of(k, STRETCH)
        reach = jnp.exp(ramp_t[k] + lead_ref[k, 0:1])
        squares = jnp.zeros((STRETCH, 1), F32)
        for q in range(g * gw // qw, (g + 1) * gw // qw):
            cols = slice(q * qw, (q + 1) * qw)
            carried = jnp.dot(
                cm_ref[rows, g * STATE : (g + 1) * STATE], inc[q], preferred_element_type=F32
            )
            gate = gate_ref[rows, cols].astype(F32)
            gated = (y_ref[rows, cols] + carried * spread(reach, q * qw, qw)) * (
                gate / (1.0 + jnp.exp(-gate))
            )
            y_ref[rows, cols] = gated
            squares = squares + jnp.sum(gated * gated, axis=1, keepdims=True)
        cols = slice(g * gw, (g + 1) * gw)
        factor = lax.rsqrt(squares / gw + 1e-05)
        normed[rows, cols] = (y_ref[rows, cols] * factor * gain_ref[:, cols].astype(F32)).astype(
            BF16
        )

    def keep_copy(r):
        return pltpu.make_async_copy(
            normed.at[:, rows_of(r, span)], tall.at[0, :, rows_of(r - base, span)], t_recv.at[r]
        )

    def mate_copy(r, start):
        return pltpu.make_async_remote_copy(
            src_ref=normed.at[:, rows_of(r, span)],
            dst_ref=tall.at[1, :, rows_of(r - start, span)],
            send_sem=t_send.at[r],
            recv_sem=m_recv.at[r],
            device_id={"ctx": mate},
            device_id_type=MESH,
        )

    def share_piece(r):
        mine = jnp.logical_and(r >= base, r < base + count)

        @pl.when(mine)
        def _():
            keep_copy(r).start()

        @pl.when(jnp.logical_not(mine))
        def _():
            mate_copy(r, mate_base).start()

    for g in range(groups):

        @pl.when(below)
        def _():
            for q in range(g * gw // qw, (g + 1) * gw // qw):
                chain(q)

        if g == groups - 1:

            @pl.when(odd == 1)
            def _():
                rest_up()

        each(blocks, lambda k: finish_group(g, k))
        lax.fori_loop(
            g * PIECES // groups,
            (g + 1) * PIECES // groups,
            lambda r, carry: (share_piece(r), carry)[1],
            0,
        )

    @pl.when(jnp.logical_and(odd == 0, z > 0))
    def _():
        rest_up()

    @pl.when(z == 0)
    def _():
        far_up()

    each(count, lambda k: keep_copy(base + k).wait())

    @pl.when(z == 0)
    def _():
        for v in range(early):
            service(v, 0, count)

    def sib_copy(o, j, c):
        return pltpu.make_async_remote_copy(
            src_ref=part.at[o, j, c, 1 - core],
            dst_ref=sib.at[o, j, c],
            send_sem=sib_send.at[o, j, c],
            recv_sem=sib_recv.at[o, j, c],
            device_id={"head": me + 1 - 2 * core},
            device_id_type=MESH,
        )

    def x_copy(o, j, c, d):
        there = lax.rem(xi + d, xs)
        return pltpu.make_async_remote_copy(
            src_ref=part.at[o, j, c, core, there],
            dst_ref=xbuf.at[d - 1, o, j, c],
            send_sem=x_send.at[d - 1, o, j, c],
            recv_sem=x_recv.at[d - 1, o, j, c],
            device_id={"head": 2 * there + core},
            device_id_type=MESH,
        )

    def z_copy(j, c):
        return pltpu.make_async_remote_copy(
            src_ref=part.at[1, j, c, core, xi],
            dst_ref=zbuf.at[j, c],
            send_sem=z_send.at[j, c],
            recv_sem=z_recv.at[j, c],
            device_id={"ctx": mate},
            device_id_type=MESH,
        )

    def multiply(o, j, c):
        def body(n):
            made = jnp.dot(
                tall[o, :, : n * span], wg[j, c, : n * span, :], preferred_element_type=F32
            ).astype(BF16)
            for h in range(peers):
                part[o, j, c, h % 2, h // 2] = made[h * owned : (h + 1) * owned]

        sized(body)
        sib_copy(o, j, c).start()

    def decode(code):
        o, u = lax.div(code, ctx * chunks), lax.rem(code, ctx * chunks)
        return o, lax.div(u, chunks), lax.rem(u, chunks)

    def chip_sum(code):
        @pl.when(code >= 0)
        def _():
            o, j, c = decode(code)
            sib_copy(o, j, c).wait_recv()
            part[o, j, c, core] = (
                part[o, j, c, core].astype(F32) + sib[o, j, c].astype(F32)
            ).astype(BF16)
            for d in range(1, xs):
                x_copy(o, j, c, d).start()

    def head_sum(code):
        @pl.when(code >= 0)
        def _():
            o, j, c = decode(code)
            sib_copy(o, j, c).wait_send()
            total = part[o, j, c, core, xi].astype(F32)
            for d in range(1, xs):
                x_copy(o, j, c, d).wait()
                total = total + xbuf[d - 1, o, j, c].astype(F32)

            @pl.when(o == 0)
            def _():
                racc[j, c] = total

            @pl.when(o == 1)
            def _():
                part[1, j, c, core, xi] = total.astype(BF16)
                z_copy(j, c).start()

    late = min(MATE_ROUND, units)
    own_kind, line_kind, side_kind = 0, 1, 2
    items = [(0, own_kind, c, 1, 0, 0) for c in range(chunks)]
    for v in range(units + 1):
        if v == late:
            waiting = [(own_kind, c) for c in range(chunks)]
            for w in range(late):
                waiting.append((line_kind, w))
                if share and w:
                    waiting.append((side_kind, w - 1))
            items += [(1, kind, i, 0, 0, int(n == 0)) for n, (kind, i) in enumerate(waiting)]
        turns = [(line_kind, v)] if v < units else []
        if share and v:
            turns.append((side_kind, v - 1))
        for n, (kind, i) in enumerate(turns):
            svc = int(n == 0 and early <= v < units)
            if v >= late:
                items += [(1, kind, i, 1, svc, 0), (0, kind, i, 0, 0, 0)]
            else:
                items.append((0, kind, i, 1, svc, 0))
    size = max(units, chunks)
    table = [
        ((((o * 3 + kind) * size + i) * 2 + new) * 2 + svc) * 2 + hold
        for o, kind, i, new, svc, hold in items
    ]
    closing = [(kind, i) for _, kind, i, *_ in items[-HEAD_LAG:]]
    settled = 0 if any(kind == own_kind for kind, _ in closing) else min(i for _, i in closing)

    def own_done(n):
        c, r = line_chunk(lax.div(n, PIECES)), lax.rem(n, PIECES)
        own_send(True, c, r, lambda node: node >= 0, True)
        own_send(False, c, r, lambda node: node >= 0, True)

    def item(t, carry):
        code = jnp.int32(table[0])
        for n in range(1, len(table)):
            code = jnp.where(t == n, table[n], code)
        hold, code = lax.rem(code, 2), lax.div(code, 2)
        svc, code = lax.rem(code, 2), lax.div(code, 2)
        new, code = lax.rem(code, 2), lax.div(code, 2)
        i, code = lax.rem(code, size), lax.div(code, size)
        kind, o = lax.rem(code, 3), lax.div(code, 3)

        @pl.when(svc == 1)
        def _():
            @pl.when(i == units - 1)
            def _():
                each(line_chunks * PIECES, own_done)
                each(settled, lambda v: service(v, 0, count, True))

            service(i, 0, count)

        @pl.when(hold == 1)
        def _():
            each(count, lambda k: mate_copy(base + k, base).wait_recv())

        _, j, at = unit_of(i)
        own = kind == own_kind
        j = jnp.where(own, z, j)
        c = jnp.where(own, i, line_chunk(at))
        if share:
            c = jnp.where(kind == side_kind, 2 * at + 1 - y, c)

        @pl.when(jnp.logical_and(own, new == 1))
        def _():
            sized(lambda n: local_copy(c, n).wait())

        if share:

            @pl.when(jnp.logical_and(kind == side_kind, new == 1))
            def _():
                each(count, lambda k: arrived(j, c, base + k))

        multiply(o, j, c)
        chip_sum(carry[CHIP_LAG - 1])
        head_sum(carry[HEAD_LAG - 1])
        return ((o * ctx + j) * chunks + c, *carry[:-1])

    none = jnp.int32(-1)
    last = lax.fori_loop(0, len(table), item, (none,) * HEAD_LAG)
    for n in range(CHIP_LAG - 1, -1, -1):
        chip_sum(last[n])

    def collect(u):
        j, c = lax.div(u, chunks), lax.rem(u, chunks)
        z_copy(j, c).wait()
        out_ref[:, rows_of(u, cw)] = (racc[j, c] + zbuf[j, c].astype(F32)).astype(BF16)

    def collect_unit(v):
        _, j, at = unit_of(v)
        collect(j * chunks + line_chunk(at))
        if share:
            collect(j * chunks + 2 * at + 1 - y)

    opened = min(line_chunks, settled)

    def collect_own(when):
        @pl.when(when)
        def _():
            each(chunks, lambda c: collect(z * chunks + c))

    if opened:
        collect_own(odd == 1)
        each(opened, collect_unit)
    for n in range(HEAD_LAG - 1, -1, -1):
        head_sum(last[n])
    each(PIECES - count, lambda k: mate_copy(mate_base + k, mate_base).wait_send())
    if units - 1 < early:
        each(line_chunks * PIECES, own_done)
        each(settled, lambda v: service(v, 0, count, True))
    lax.fori_loop(settled, units, lambda v, carry: (service(v, 0, count, True), carry)[1], 0)

    @pl.when(above)
    def _():
        for q in range(QUARTERS):
            state_copy(q).wait_send()

    collect_own(odd == 0 if opened else odd >= 0)
    lax.fori_loop(opened, units, lambda v, carry: (collect_unit(v), carry)[1], 0)


def shards(
    sizes,
    head_input,
    gate_input,
    input_map,
    output_map,
    step_size,
    decays,
    bypass_scale,
    norm_gain,
    out_weight,
):
    lanes, ctx, peers = sizes
    tokens, width = head_input.shape
    heads = step_size.shape[0]
    blocks = tokens // STRETCH
    depth, cols = out_weight.shape
    cw = min(cols, 256)
    chunks = cols // cw
    owned, xs = tokens // peers, peers // 2
    most = max(SPLIT, PIECES - SPLIT, LAST_SPLIT, PIECES - LAST_SPLIT)
    dma = pltpu.SemaphoreType.DMA
    vmem = pl.BlockSpec(memory_space=pltpu.VMEM)
    anywhere = pl.BlockSpec(memory_space=pl.ANY)
    return pl.pallas_call(
        functools.partial(layer, sizes),
        out_shape=jax.ShapeDtypeStruct((owned, ctx * cols), BF16),
        in_specs=[anywhere] * 4 + [vmem] * 4 + [anywhere],
        out_specs=vmem,
        scratch_shapes=[
            pltpu.VMEM(head_input.shape, BF16),
            pltpu.VMEM(gate_input.shape, BF16),
            pltpu.VMEM(input_map.shape, BF16),
            pltpu.VMEM(output_map.shape, BF16),
            pltpu.VMEM((ctx, chunks, most * depth // PIECES, cw), BF16),
            pltpu.VMEM((2, ctx, chunks, 2, xs, owned, cw), BF16),
            pltpu.VMEM((2, ctx, chunks, xs, owned, cw), BF16),
            pltpu.VMEM((max(xs - 1, 1), 2, ctx, chunks, owned, cw), BF16),
            pltpu.VMEM((ctx, chunks, owned, cw), F32),
            pltpu.VMEM((ctx, chunks, owned, cw), BF16),
            pltpu.VMEM((tokens, width), F32),
            pltpu.VMEM((STATE, width), F32),
            pltpu.VMEM((blocks, STATE, width), BF16),
            pltpu.VMEM((QUARTERS, STATE, width // QUARTERS), BF16),
            pltpu.VMEM((QUARTERS, STATE, width // QUARTERS), BF16),
            pltpu.VMEM((tokens, width), BF16),
            pltpu.VMEM((2, tokens, most * depth // PIECES), BF16),
            pltpu.VMEM((heads, width), BF16),
            pltpu.VMEM((blocks, STRETCH, heads), F32),
            pltpu.VMEM((blocks, heads, STRETCH), F32),
            pltpu.VMEM((blocks, 8, heads), F32),
            pltpu.VMEM((8, heads), F32),
            dma((4,)),
            dma((chunks,)),
            dma((PIECES,)),
            dma((ctx, chunks, PIECES)),
            dma((ctx, chunks, PIECES)),
            dma((ctx, chunks, PIECES)),
            dma((ctx, chunks, PIECES)),
            dma((QUARTERS,)),
            dma((QUARTERS,)),
            dma((PIECES,)),
            dma((PIECES,)),
            dma((2, ctx, chunks)),
            dma((2, ctx, chunks)),
            dma((max(xs - 1, 1), 2, ctx, chunks)),
            dma((max(xs - 1, 1), 2, ctx, chunks)),
            dma((ctx, chunks)),
            dma((ctx, chunks)),
        ],
        compiler_params=pltpu.CompilerParams(
            collective_id=0, has_side_effects=True, vmem_limit_bytes=60 << 20
        ),
    )(
        head_input,
        gate_input,
        input_map,
        output_map,
        step_size,
        decays,
        bypass_scale.reshape(1, heads),
        norm_gain.reshape(1, width),
        out_weight,
    )


def solution(mesh):
    sizes = (mesh.shape["group"], mesh.shape["ctx"], mesh.shape["head"])
    return jax.shard_map(
        functools.partial(shards, sizes),
        mesh=mesh,
        in_specs=(
            P(("group", "ctx"), "head"),
            P(("group", "ctx"), "head"),
            P(("group", "ctx"), "head"),
            P(("group", "ctx"), "head"),
            P("head", ("group", "ctx")),
            P("head", ("group", "ctx")),
            P("head"),
            P("head"),
            P("head", "ctx"),
        ),
        out_specs=P(("group", "ctx", "head"), None),
        check_vma=False,
    )
```
